32 devices in a mesh: section: 1, dp: 32 (over z, y, x, core).
Axes of the slice: x: 2, y: 2, z: 4, core: 2. Of those that a mesh axis runs over, the one named last changes fastest.
Arguments:
- tokens: bfloat16 [4096, 8192], P('dp'), may hold values from -6 to 6
- blocks_in: bfloat16 [1, 160, 128, 128], P('section', 'dp'), may hold values from -0.078125 to 0.078125
- blocks_out: bfloat16 [1, 160, 128, 128], P('section', 'dp'), may hold values from -0.3125 to 0.3125
- pos_in: int32 [1, 160], P('section', 'dp'), may hold values from 0 to 256, as said below
- pos_out: int32 [1, 160], P('section', 'dp'), may hold values from 0 to 256, as said below
- cotangent: bfloat16 [4096, 8192], P('dp'), may hold values from -0.08984375 to 0.08984375
Outputs:
- grad_in: bfloat16 [1, 160, 128, 128], P('section', 'dp')
- grad_out: bfloat16 [1, 160, 128, 128], P('section', 'dp')
The draws below stay inside these ranges and needn't reach their ends.
Inputs may be any that keep to these rules, and one draw needn't show every extreme that they name: For each layer the first k slots (k from 110 to 160) hold distinct block numbers and the other slots hold 256, marking an empty slot; in each of pos_in and pos_out some layer fills all 160 slots. `pos_out`: as for pos_in, drawn independently.
All inputs are finite; a program needn't handle non-finite values.
Results may differ from the reference program's by a relative error of at most 0.023.
Values may be sent and summed in bfloat16 or wider, within the bound.
A program may use at most 128 MiB of HBM per device.

```python
import jax
import jax.numpy as jnp
from jax import lax

D = 8192
RANK = 512
BLOCK = 128
CAP = 160
LIVE_LO = 110
NBLK = 256
TOK_DEV = 128
LAYERS = 1
TOKENS = 4096
N_DP = 32


def block_places(key, which):
    base = jax.random.fold_in(key, 77)
    count_key = jax.random.fold_in(jax.random.fold_in(base, 1), which)
    full_key = jax.random.fold_in(jax.random.fold_in(base, 2), which)
    perm_key = jax.random.fold_in(jax.random.fold_in(base, 3), which)
    counts = jax.random.randint(count_key, (LAYERS,), LIVE_LO, CAP + 1)
    filled = jax.random.randint(full_key, (), 0, LAYERS)
    counts = jnp.where(jnp.arange(LAYERS) == filled, CAP, counts)
    layer_keys = jax.random.split(perm_key, LAYERS)
    perms = jax.vmap(lambda kk: jax.random.permutation(kk, NBLK)[:CAP])(layer_keys)
    slots = jnp.arange(CAP)
    return jnp.where(slots[None, :] < counts[:, None], perms, NBLK).astype(jnp.int32)


def draw_pos_in(key, part):
    return block_places(key, 0)


def draw_pos_out(key, part):
    return block_places(key, 1)


def block_levels(stream_key, dims, cuts, least, largest):
    gain = 1.0
    for dim, blocks in cuts:
        heights = jax.random.uniform(jax.random.fold_in(jax.random.fold_in(stream_key, 6), dim), (blocks,), jnp.float32, least / len(cuts), largest / len(cuts))
        gain = gain * jnp.repeat(jnp.exp(heights), dims[dim] // blocks).reshape((-1,) + (1,) * (len(dims) - 1 - dim))
    return gain


def centred(own_key, shape, deviation, limit, pieces=(), kind=jnp.bfloat16):
    values = deviation * jax.random.normal(own_key, shape, jnp.float32)
    if pieces:
        values = values * block_levels(own_key, shape, pieces, -0.22, 0.18)
    return jnp.clip(values, -limit, limit).astype(kind)


def setup_inputs(seed: int = 0) -> dict:
    key_list = jax.random.split(jax.random.key(seed), 7)
    return {
        "tokens": centred(key_list[0], (TOKENS, D), 1.0, 6.0, ((0, 32),)),
        "blocks_in": centred(key_list[1], (LAYERS, CAP, BLOCK, BLOCK), (CAP * BLOCK * BLOCK // RANK) ** -0.5, 0.078125, ((1, 32),)),
        "blocks_out": centred(key_list[2], (LAYERS, CAP, BLOCK, BLOCK), (CAP * BLOCK * BLOCK // D) ** -0.5, 0.3125, ((1, 32),)),
        "pos_in": draw_pos_in(jax.random.fold_in(key_list[6], 71), 0),
        "pos_out": draw_pos_out(jax.random.fold_in(key_list[6], 71), 0),
        "cotangent": centred(key_list[5], (TOKENS, D), 0.015625, 0.08984375, ((0, 32),)),
    }


EPS = 1e-05

def expand(blocks, places, rows_b, cols_b):
    flat = jnp.zeros((rows_b * cols_b, BLOCK, BLOCK), blocks.dtype)
    flat = flat.at[places].set(blocks, mode='drop')
    return flat.reshape(rows_b, cols_b, BLOCK, BLOCK).transpose(0, 2, 1, 3).reshape(rows_b * BLOCK, cols_b * BLOCK)

def pack(dense, places, rows_b, cols_b):
    blocks = dense.reshape(rows_b, BLOCK, cols_b, BLOCK).transpose(0, 2, 1, 3).reshape(rows_b * cols_b, BLOCK, BLOCK)
    return jnp.take(blocks, places, axis=0, mode='fill', fill_value=0.0)

def norm_parts(hidden):
    wide = hidden.astype(jnp.float32)
    scale = jnp.sqrt(lax.optimization_barrier(jnp.mean(wide * wide, axis=-1, keepdims=True)) + EPS)
    return (wide, scale)

def device_sums(left, right, places, rows_b, cols_b):
    left_dev = left.reshape(N_DP, TOK_DEV, left.shape[1])
    right_dev = right.reshape(N_DP, TOK_DEV, right.shape[1])

    def step(total, pair):
        part = lax.dot_general(pair[0], pair[1], (((0,), (0,)), ((), ())), preferred_element_type=jnp.float32)
        packed = pack(part, places, rows_b, cols_b).astype(jnp.bfloat16)
        packed = lax.optimization_barrier(packed)
        return (total + packed.astype(jnp.float32), None)
    init = jnp.zeros((places.shape[0], BLOCK, BLOCK), jnp.float32)
    total, _ = lax.scan(step, init, (left_dev, right_dev))
    return total

def reference(tokens, blocks_in, blocks_out, pos_in, pos_out, cotangent):
    rows_d = D // BLOCK
    rows_k = RANK // BLOCK
    mats_a = [expand(blocks_in[l], pos_in[l], rows_d, rows_k) for l in range(LAYERS)]
    mats_b = [expand(blocks_out[l], pos_out[l], rows_k, rows_d) for l in range(LAYERS)]
    states = [tokens]
    for l in range(LAYERS):
        wide, scale = norm_parts(states[l])
        normed = (wide / scale).astype(jnp.bfloat16)
        pre = jnp.dot(normed, mats_a[l], preferred_element_type=jnp.float32)
        act = (pre * jax.nn.sigmoid(pre)).astype(jnp.bfloat16)
        states.append((wide + jnp.dot(act, mats_b[l], preferred_element_type=jnp.float32)).astype(jnp.bfloat16))
    upstream = cotangent
    grads_in = [None] * LAYERS
    grads_out = [None] * LAYERS
    for l in reversed(range(LAYERS)):
        wide, scale = norm_parts(states[l])
        unit = wide / scale
        normed = unit.astype(jnp.bfloat16)
        pre = jnp.dot(normed, mats_a[l], preferred_element_type=jnp.float32)
        sig = jax.nn.sigmoid(pre)
        act = (pre * sig).astype(jnp.bfloat16)
        dact = lax.dot_general(upstream, mats_b[l], (((1,), (1,)), ((), ())), preferred_element_type=jnp.float32)
        dpre = (dact * sig * (1.0 + pre * (1.0 - sig))).astype(jnp.bfloat16)
        dnorm = lax.dot_general(dpre, mats_a[l], (((1,), (1,)), ((), ())), preferred_element_type=jnp.float32)
        grads_in[l] = device_sums(normed, dpre, pos_in[l], rows_d, rows_k).astype(jnp.bfloat16)
        grads_out[l] = device_sums(act, upstream, pos_out[l], rows_k, rows_d).astype(jnp.bfloat16)
        inner = lax.optimization_barrier(jnp.mean(dnorm * unit, axis=-1, keepdims=True))
        upstream = (upstream.astype(jnp.float32) + (dnorm - unit * inner) / scale).astype(jnp.bfloat16)
    return (jnp.stack(grads_in), jnp.stack(grads_out))
```

```python
import functools

import jax
import jax.numpy as jnp
from jax import lax
from jax.experimental import pallas as pl
from jax.experimental.pallas import tpu as pltpu
from jax.sharding import PartitionSpec as P

D = 8192
RANK = 512
BLOCK = 128
MICRO = 2


EPS = 1e-05


def from_behind(block, axis, distance):
    devices = range(lax.axis_size(axis))
    route = [(i - distance, i) for i in devices if i - distance in devices]
    return lax.ppermute(block, axis, route)


def expand(blocks, places, rows_b, cols_b):
    flat = jnp.zeros((rows_b * cols_b, BLOCK, BLOCK), blocks.dtype)
    flat = flat.at[places].set(blocks, mode="drop")
    return (
        flat.reshape(rows_b, cols_b, BLOCK, BLOCK)
        .transpose(0, 2, 1, 3)
        .reshape(rows_b * BLOCK, cols_b * BLOCK)
    )


def slot_grads(left, right, places, rows_b, cols_b):
    count = left.shape[0]
    valid = places < rows_b * cols_b
    row_block = jnp.where(valid, places // cols_b, 0).astype(jnp.int32)
    col_block = jnp.where(valid, places % cols_b, 0).astype(jnp.int32)
    left_blocks = jnp.take(left.reshape(count, rows_b, BLOCK), row_block, axis=1)
    right_blocks = jnp.take(right.reshape(count, cols_b, BLOCK), col_block, axis=1)
    result = jnp.einsum(
        "tjb,tjc->jbc", left_blocks, right_blocks, preferred_element_type=jnp.float32
    )
    return jnp.where(valid[:, None, None], result, 0.0)


def norm_parts(hidden):
    wide = hidden.astype(jnp.float32)
    scale = jnp.sqrt(jnp.mean(wide * wide, axis=-1, keepdims=True) + EPS)
    return (wide, scale)


def forward_layer(hidden, mat_a, mat_b):
    wide, scale = norm_parts(hidden)
    normed = (wide / scale).astype(jnp.bfloat16)
    pre = jnp.dot(normed, mat_a, preferred_element_type=jnp.float32)
    act = (pre * jax.nn.sigmoid(pre)).astype(jnp.bfloat16)
    return (wide + jnp.dot(act, mat_b, preferred_element_type=jnp.float32)).astype(jnp.bfloat16)


def backward_layer(hidden, upstream, mat_a, mat_b):
    wide, scale = norm_parts(hidden)
    unit = wide / scale
    normed = unit.astype(jnp.bfloat16)
    pre = jnp.dot(normed, mat_a, preferred_element_type=jnp.float32)
    sig = jax.nn.sigmoid(pre)
    act = (pre * sig).astype(jnp.bfloat16)
    dact = lax.dot_general(
        upstream, mat_b, (((1,), (1,)), ((), ())), preferred_element_type=jnp.float32
    )
    dpre = (dact * sig * (1.0 + pre * (1.0 - sig))).astype(jnp.bfloat16)
    dnorm = lax.dot_general(
        dpre, mat_a, (((1,), (1,)), ((), ())), preferred_element_type=jnp.float32
    )
    inner = jnp.mean(dnorm * unit, axis=-1, keepdims=True)
    earlier = (upstream.astype(jnp.float32) + (dnorm - unit * inner) / scale).astype(jnp.bfloat16)
    return (earlier, normed, dpre, act)


def store(stack, value, picked, active):
    updated = lax.dynamic_update_slice_in_dim(stack, value[None], picked, 0)
    return jnp.where(active, updated, stack)


def per_device(tokens, blocks_in, blocks_out, pos_in, pos_out, cotangent):
    sections = lax.axis_size("section")
    here = lax.axis_index("section")
    rows_d = D // BLOCK
    rows_k = RANK // BLOCK
    full_in, full_out, all_in, all_out = (
        lax.all_gather(blocks_in, "dp", axis=1, tiled=True),
        lax.all_gather(blocks_out, "dp", axis=1, tiled=True),
        lax.all_gather(pos_in, "dp", axis=1, tiled=True),
        lax.all_gather(pos_out, "dp", axis=1, tiled=True),
    )
    mat_a = expand(full_in[0], all_in[0], rows_d, rows_k)
    mat_b = expand(full_out[0], all_out[0], rows_k, rows_d)
    micro_rows = tokens.shape[0] // MICRO
    turns = MICRO + sections - 1
    saved = jnp.zeros((MICRO, micro_rows, D), jnp.bfloat16)
    carried = jnp.zeros((micro_rows, D), jnp.bfloat16)
    for turn in range(turns):
        micro = turn - here
        active = (micro >= 0) & (micro < MICRO)
        picked = jnp.clip(micro, 0, MICRO - 1)
        first = lax.dynamic_slice_in_dim(tokens, picked * micro_rows, micro_rows, 0)
        entering = jnp.where(here == 0, first, carried)
        saved = store(saved, entering, picked, active)
        if turn < turns - 1:
            leaving = lax.cond(
                active, lambda x: forward_layer(x, mat_a, mat_b), lambda x: x, entering
            )
            carried = from_behind(leaving, "section", 1)
    kept_normed = jnp.zeros((MICRO, micro_rows, D), jnp.bfloat16)
    kept_dpre = jnp.zeros((MICRO, micro_rows, RANK), jnp.bfloat16)
    kept_act = jnp.zeros((MICRO, micro_rows, RANK), jnp.bfloat16)
    kept_upper = jnp.zeros((MICRO, micro_rows, D), jnp.bfloat16)
    carried_grad = jnp.zeros((micro_rows, D), jnp.bfloat16)
    for turn in range(turns):
        micro = turn - (sections - 1 - here)
        active = (micro >= 0) & (micro < MICRO)
        picked = jnp.clip(micro, 0, MICRO - 1)
        last = lax.dynamic_slice_in_dim(cotangent, picked * micro_rows, micro_rows, 0)
        upstream = jnp.where(here == sections - 1, last, carried_grad)
        hidden = lax.dynamic_index_in_dim(saved, picked, 0, keepdims=False)

        def run_layer():
            return backward_layer(hidden, upstream, mat_a, mat_b)

        def skip_layer():
            return (
                upstream,
                jnp.zeros((micro_rows, D), jnp.bfloat16),
                jnp.zeros((micro_rows, RANK), jnp.bfloat16),
                jnp.zeros((micro_rows, RANK), jnp.bfloat16),
            )

        earlier, normed, dpre, act = lax.cond(active, run_layer, skip_layer)
        kept_normed = store(kept_normed, normed, picked, active)
        kept_dpre = store(kept_dpre, dpre, picked, active)
        kept_act = store(kept_act, act, picked, active)
        kept_upper = store(kept_upper, upstream, picked, active)
        if turn < turns - 1:
            carried_grad = from_behind(earlier, "section", -1)
    all_rows = MICRO * micro_rows
    terms_in = slot_grads(
        kept_normed.reshape(all_rows, D),
        kept_dpre.reshape(all_rows, RANK),
        all_in[0],
        rows_d,
        rows_k,
    )[None]
    terms_out = slot_grads(
        kept_act.reshape(all_rows, RANK),
        kept_upper.reshape(all_rows, D),
        all_out[0],
        rows_k,
        rows_d,
    )[None]
    sums_in, sums_out = (
        lax.psum_scatter(
            terms_in.astype(jnp.bfloat16), "dp", scatter_dimension=1, tiled=True
        ).astype(jnp.float32),
        lax.psum_scatter(
            terms_out.astype(jnp.bfloat16), "dp", scatter_dimension=1, tiled=True
        ).astype(jnp.float32),
    )
    return (sums_in.astype(jnp.bfloat16), sums_out.astype(jnp.bfloat16))


SLICES = 2
PLANE = 1
CHUNK = 1024


class Place:
    def __init__(self, devices):
        me = lax.axis_index("dp")
        self.depth = devices // 8
        self.me = me
        self.core = me % 2
        self.chip = me // 2
        x = self.chip % 2
        y = (self.chip // 2) % 2
        self.z = self.chip // 4
        dx = 1 - 2 * x
        dy = 2 * (1 - 2 * y)
        first = (1 - self.core) * dx + self.core * dy
        second = (1 - self.core) * dy + self.core * dx
        self.own = self.chip % 4
        self.near = self.own + first
        self.far = self.own + second
        self.diag = self.own + first + second
        self.sibling = me + 1 - 2 * self.core
        self.first = me + 2 * first
        self.second = me + 2 * second
        self.above = me + 8
        self.below = me - 8
        self.has_above = self.z + 1 < self.depth
        self.has_below = self.z >= 1

    def knock(self):
        barrier = pltpu.get_barrier_semaphore()

        def signal(peer):
            pl.semaphore_signal(
                barrier, inc=1, device_id={"dp": peer}, device_id_type=pl.DeviceIdType.MESH
            )

        for peer in (self.sibling, self.first, self.second):
            signal(peer)
        pl.when(self.has_above)(lambda: signal(self.above))
        pl.when(self.has_below)(lambda: signal(self.below))

        peers = 3 + self.has_above.astype(jnp.int32) + self.has_below.astype(jnp.int32)
        return lambda: pl.semaphore_wait(barrier, peers)


def remote(src, dst, send, recv, peer):
    return pltpu.make_async_remote_copy(
        src_ref=src,
        dst_ref=dst,
        send_sem=send,
        recv_sem=recv,
        device_id={"dp": peer},
        device_id_type=pl.DeviceIdType.MESH,
    )


class Layout:
    def __init__(self, devices, per):
        self.per = per
        self.depth = devices // 8
        self.sizes = (4 * (per - PLANE), 4 * PLANE)
        self.plane = 16 * per
        self.total = self.depth * self.plane

    def start(self, part, z, p):
        line, odd = self.sizes
        return z * self.plane + (p * line if part == 0 else 4 * line + p * odd)

    def piece(self, buf, k, part, z, p):
        span = pl.ds(self.start(part, z, p), self.sizes[part])
        return buf.at[span] if k is None else buf.at[k, span]

    def level(self, buf, k, z):
        line, odd = self.sizes
        span = pl.ds(z * self.plane + 4 * line, 4 * odd)
        return buf.at[span] if k is None else buf.at[k, span]


def fused_kernel(devices, pos_in, pos_out, own_in, own_out, tokens, cotangent, out_in, out_out,
                 full, stage, rows_h, rows_g, mats, grads, inverse,
                 tags, table, table_s, begin, begin_s, mid,
                 held, from_second, from_first, from_below, from_above, final, twin, flat,
                 load_sems, send_sems, pair_sems, twin_sems, tag_sems, gather_sems, level_sems,
                 second_sems, first_sems, below_sems, above_sems):
    at = Place(devices)
    depth = at.depth
    core = at.core
    per = own_in.shape[0]
    lay = Layout(devices, per)
    count, width = tokens.shape
    size = full[0].shape[1]
    half = BLOCK // 2
    rows_k = RANK // BLOCK
    rows_d = width // BLOCK
    blocks = rows_k * rows_d
    ranks = rows_k * size
    chunks = width // CHUNK
    sends = []

    def send(src, dst, recv, peer, present=None):
        remote(src, dst, send_sems.at[len(sends)], recv, peer).start()
        rows, whole = src.shape[0], src.dtype == jnp.int32
        if whole and len(src.shape) == 2:
            sends.append((lambda: tags.at[0], present))
        elif whole:
            sends.append((lambda: tags.at[pl.ds(0, rows)], present))
        else:
            sends.append((lambda: full[0].at[pl.ds(0, rows)], present))

    def got(buf, sem):
        remote(buf, buf, send_sems.at[0], sem, at.sibling).wait_recv()

    wait_peers = at.knock()

    own_rows = pl.ds(pl.multiple_of(core * count, count), count)
    local = [
        pltpu.make_async_copy(tokens, rows_h.at[own_rows], load_sems.at[0]),
        pltpu.make_async_copy(cotangent, rows_g.at[own_rows], load_sems.at[1]),
    ]
    for copy in local:
        copy.start()

    def offset(part, j):
        return 2 * j if part == 0 else 2 * (j - (per - PLANE))

    def part_of(j):
        return 0 if j < per - PLANE else 1

    lanes = lax.broadcasted_iota(jnp.int32, tags.shape[1:], 1)
    row = jnp.full(tags.shape[1:], blocks, jnp.int32)
    for j in range(per):
        row = jnp.where(lanes == 2 * j, pos_in[0, j], row)
        row = jnp.where(lanes == 2 * j + 1, pos_out[0, j] + blocks + 1, row)
    tags[at.me] = row

    for j in range(per):
        part = part_of(j)
        base = lay.start(part, at.z, at.own) + core * (lay.sizes[part] // 2) + offset(part, j)
        flat[0] = own_in[j].T
        flat[1] = own_out[j]
        for k in range(SLICES):
            keep = pl.ds(pl.multiple_of(core * half + k * size, size), size)
            give = pl.ds(pl.multiple_of((1 - core) * half + k * size, size), size)
            for m in range(2):
                full[k][base + m] = flat[m, keep, :]
                stage[k, 2 * j + m] = flat[m, give, :]
    for k in range(SLICES):
        full[k][lay.total] = jnp.zeros((size, BLOCK), jnp.bfloat16)
        for m in range(2):
            grads[k][m * (blocks + 1) + blocks] = jnp.zeros((size, BLOCK), jnp.bfloat16)

    wait_peers()

    def pair(k, start):
        for part in range(2):
            n = lay.sizes[part] // 2
            base = lay.start(part, at.z, at.own) + core * n
            first = 0 if part == 0 else lay.sizes[0] // 2
            src, dst = stage.at[k, pl.ds(first, n)], full[k].at[pl.ds(base, n)]
            if start:
                send(src, dst, pair_sems.at[k, part], at.sibling)
            else:
                got(src, pair_sems.at[k, part])

    send(tags.at[at.me], tags.at[at.me], tag_sems.at[2 * depth * 4], at.sibling)
    for k in range(SLICES):
        pair(k, True)

    def tag_piece(z, p):
        return tags.at[pl.ds(2 * (4 * z + p), 2)]

    def push(k, part, z, p, peer, present=None):
        if k == 0 and part == 0:
            piece = tag_piece(z, p)
            send(piece, piece, tag_sems.at[4 * z + p], peer, present)
        piece = lay.piece(full[k], None, part, z, p)
        send(piece, piece, gather_sems.at[k, part, 4 * z + p], peer, present)

    def arrived(k, part, z, p):
        if k == 0 and part == 0:
            got(tag_piece(z, p), tag_sems.at[4 * z + p])
        got(lay.piece(full[k], None, part, z, p), gather_sems.at[k, part, 4 * z + p])

    def when(cond, run):
        pl.when(cond)(run)

    def up_push(k, z, p, present):
        when(at.has_above, lambda: push(k, 0, z, p, at.above, present))

    def down_push(k, z, p, present):
        when(at.has_below, lambda: push(k, 0, z, p, at.below, present))

    def gather_own(k):
        pair(k, False)
        if k == 0:
            got(tags.at[at.me], tag_sems.at[2 * depth * 4])
        push(k, 0, at.z, at.own, at.second)
        push(k, 0, at.z, at.own, at.first)
        up_push(k, at.z, at.own, lambda: at.has_above)
        down_push(k, at.z, at.own, lambda: at.has_below)
        push(k, 1, at.z, at.own, at.second)
        push(k, 1, at.z, at.own, at.first)

    def near_own(k):
        for part in range(2):
            arrived(k, part, at.z, at.near)
            push(k, part, at.z, at.near, at.second)

    def line(k, d):
        def below():
            z = at.z - d
            arrived(k, 0, z, at.own)
            up_push(k, z, at.own, lambda: at.has_above & (at.z >= d))
            push(k, 0, z, at.own, at.second, lambda: at.z >= d)
            push(k, 0, z, at.own, at.first, lambda: at.z >= d)

        def above():
            z = at.z + d
            arrived(k, 0, z, at.own)
            down_push(k, z, at.own, lambda: at.has_below & (at.z + d < depth))
            push(k, 0, z, at.own, at.second, lambda: at.z + d < depth)
            push(k, 0, z, at.own, at.first, lambda: at.z + d < depth)

        when(at.z >= d, below)
        when(at.z + d < depth, above)

    def near_line(k, d):
        def below():
            arrived(k, 0, at.z - d, at.near)
            push(k, 0, at.z - d, at.near, at.second, lambda: at.z >= d)

        def above():
            arrived(k, 0, at.z + d, at.near)
            push(k, 0, at.z + d, at.near, at.second, lambda: at.z + d < depth)

        when(at.z >= d, below)
        when(at.z + d < depth, above)

    def push_level(k, z, peer, to_above, present):
        piece = lay.level(full[k], None, z)
        send(piece, piece, level_sems.at[k, z], peer, present)

    def plane_own(k):
        for part in range(2):
            for p in (at.far, at.diag):
                arrived(k, part, at.z, p)
        when(at.has_above, lambda: push_level(k, at.z, at.above, True, lambda: at.has_above))
        when(at.has_below, lambda: push_level(k, at.z, at.below, False, lambda: at.has_below))

    def plane(k, d):
        def below():
            got(lay.level(full[k], None, at.z - d), level_sems.at[k, at.z - d])
            when(
                at.has_above,
                lambda: push_level(k, at.z - d, at.above, True, lambda: at.has_above & (at.z >= d)),
            )

        def above():
            got(lay.level(full[k], None, at.z + d), level_sems.at[k, at.z + d])
            when(
                at.has_below,
                lambda: push_level(
                    k, at.z + d, at.below, False, lambda: at.has_below & (at.z + d < depth)
                ),
            )

        when(at.z >= d, below)
        when(at.z + d < depth, above)

    def side(k):
        for d in range(1, depth):

            def below(d=d):
                for p in (at.far, at.diag):
                    arrived(k, 0, at.z - d, p)

            def above(d=d):
                for p in (at.far, at.diag):
                    arrived(k, 0, at.z + d, p)

            when(at.z >= d, below)
            when(at.z + d < depth, above)

    def load_rows():
        swap = [
            remote(tokens, rows_h.at[own_rows], send_sems.at[len(sends)], load_sems.at[2], at.sibling),
            remote(cotangent, rows_g.at[own_rows], send_sems.at[len(sends) + 1], load_sems.at[3], at.sibling),
        ]
        for copy, src in zip(swap, (tokens, cotangent)):
            copy.start()
            sends.append((lambda src=src: src, None))
        return swap

    def scales():
        total = jnp.zeros((2 * count, BLOCK), jnp.float32)
        for i in range(0, width, BLOCK):
            wide = rows_h[:, i : i + BLOCK].astype(jnp.float32)
            total += wide * wide
        scale = jnp.sqrt(jnp.sum(total, axis=-1, keepdims=True) / width + EPS)
        inverse[...] = jnp.broadcast_to(1.0 / scale, inverse.shape)

    def tables():
        table[...] = tags[:, 0, :]
        copy = pltpu.make_async_copy(table, table_s, load_sems.at[4])
        copy.start()
        copy.wait()
        shape = begin.shape
        numbers = lax.broadcasted_iota(jnp.int32, shape, 0) * BLOCK
        numbers += lax.broadcasted_iota(jnp.int32, shape, 1)

        def scan(dev, found):
            z, p, which = dev // 8, (dev // 2) % 4, dev % 2
            for lane in range(2 * per):
                part = part_of(lane // 2)
                first = 0 if part == 0 else lay.sizes[0] // 2
                entry = lay.start(part, z, p) + which * (lay.sizes[part] // 2) + lane - first
                found = jnp.where(numbers == table_s[dev, lane], entry, found)
            return found

        begin[...] = lax.fori_loop(0, devices, scan, jnp.full(shape, lay.total, jnp.int32))
        copy = pltpu.make_async_copy(begin, begin_s, load_sems.at[4])
        copy.start()
        copy.wait()

    def expand(k, m):
        def step(r, carry):
            into = pl.ds(pl.multiple_of(r * BLOCK, BLOCK), BLOCK)
            for c in range(rows_k):
                b = r * rows_k + c if m == 0 else blocks + 1 + c * rows_d + r
                mats[m, c * size : (c + 1) * size, into] = full[k][begin_s[b // BLOCK, b % BLOCK]]
            return carry

        lax.fori_loop(0, rows_d, step, 0)

    def product(m):
        rows = rows_h if m == 0 else rows_g
        total = jnp.zeros((2 * count, ranks), jnp.float32)
        for i in range(0, width, CHUNK):
            total += lax.dot_general(
                rows[:, i : i + CHUNK], mats[m, :, i : i + CHUNK],
                (((1,), (1,)), ((), ())), preferred_element_type=jnp.float32,
            )
        return total

    def middle(k):
        pre = product(0) * inverse[:, :1]
        dact = product(1)
        sig = jax.nn.sigmoid(pre)
        dpre = dact * sig * (1.0 + pre * (1.0 - sig))
        mid[0] = (dpre * inverse[:, :1]).astype(jnp.bfloat16)
        mid[1] = (pre * sig).astype(jnp.bfloat16)

    def outer(k, m):
        rows = rows_h if m == 0 else rows_g

        def step(i, carry):
            into = pl.ds(pl.multiple_of(i * CHUNK, CHUNK), CHUNK)
            part = lax.dot_general(
                mid[m], rows[:, into], (((0,), (0,)), ((), ())), preferred_element_type=jnp.float32
            ).astype(jnp.bfloat16)
            for r in range(CHUNK // BLOCK):
                col = i * (CHUNK // BLOCK) + r
                for c in range(rows_k):
                    b = col * rows_k + c if m == 0 else blocks + 1 + c * rows_d + col
                    grads[k][b] = part[c * size : (c + 1) * size, r * BLOCK : (r + 1) * BLOCK]
            return carry

        lax.fori_loop(0, chunks, step, 0)

    def fill(k, part, z, p, terms, into=None):
        n = lay.sizes[part] // 2
        first = 0 if part == 0 else lay.sizes[0] // 2
        target = held if into is None else into
        base = lay.start(part, z, p)

        def step(which, carry):
            dev = 2 * (4 * z + p) + which
            for i in range(n):
                entry = base + which * n + i
                value = grads[k][table_s[dev, first + i]]
                if terms:
                    value = value.astype(jnp.float32)
                    for term in terms:
                        value += term[k, entry].astype(jnp.float32)
                    value = value.astype(jnp.bfloat16)
                if into is None:
                    target[k, entry] = value
                else:
                    target[k, 2 * first + which * n + i] = value
            return carry

        lax.fori_loop(0, 2, step, 0)

    def give(k, part, z, p, buf, sems, peer, present=None):
        src = lay.piece(held, k, part, z, p)
        send(src, lay.piece(buf, k, part, z, p), sems.at[k, part, 4 * z + p], peer, present)

    def take(k, part, z, p, buf, sems):
        got(lay.piece(buf, k, part, z, p), sems.at[k, part, 4 * z + p])

    def reduce_levels(k):
        for d in range(depth - 1, 0, -1):

            def upward(d=d):
                z = at.z + d

                def own():
                    for p in range(4):
                        fill(k, 1, z, p, [])

                def summed():
                    got(lay.level(from_below, k, z), below_sems.at[k, 1, z])
                    for p in range(4):
                        fill(k, 1, z, p, [from_below])

                when(jnp.logical_not(at.has_below), own)
                when(at.has_below, summed)
                send(
                    lay.level(held, k, z), lay.level(from_below, k, z), below_sems.at[k, 1, z],
                    at.above, lambda: at.z + d < depth,
                )

            def downward(d=d):
                z = at.z - d

                def own():
                    for p in range(4):
                        fill(k, 1, z, p, [])

                def summed():
                    got(lay.level(from_above, k, z), above_sems.at[k, 1, z])
                    for p in range(4):
                        fill(k, 1, z, p, [from_above])

                when(jnp.logical_not(at.has_above), own)
                when(at.has_above, summed)
                send(
                    lay.level(held, k, z), lay.level(from_above, k, z), above_sems.at[k, 1, z],
                    at.below, lambda: at.z >= d,
                )

            when(at.z + d < depth, upward)
            when(at.z >= d, downward)

    def beside(run):
        when(at.has_below & at.has_above, lambda: run([from_below, from_above]))
        when(at.has_below & jnp.logical_not(at.has_above), lambda: run([from_below]))
        when(at.has_above & jnp.logical_not(at.has_below), lambda: run([from_above]))

    def order():
        return [(at.z + d) % depth for d in (2, 1, 3, 0)][-depth:] if depth == 4 else [
            (at.z + d) % depth for d in range(depth - 1, -1, -1)
        ]

    def reduce_second(k):
        for z in order():
            for p in (at.diag, at.far):
                fill(k, 0, z, p, [])
                give(k, 0, z, p, from_second, second_sems, at.second)

    def level_sums(k):
        when(at.has_below, lambda: got(lay.level(from_below, k, at.z), below_sems.at[k, 1, at.z]))
        when(at.has_above, lambda: got(lay.level(from_above, k, at.z), above_sems.at[k, 1, at.z]))

        def run(terms):
            for p in (at.diag, at.far):
                fill(k, 1, at.z, p, terms)

        beside(run)
        for p in (at.diag, at.far):
            give(k, 1, at.z, p, from_second, second_sems, at.second)

    def reduce_first(k):
        for z in order():
            take(k, 0, z, at.near, from_second, second_sems)
            fill(k, 0, z, at.near, [from_second])
            give(k, 0, z, at.near, from_first, first_sems, at.first)

    def level_first(k):
        take(k, 1, at.z, at.near, from_second, second_sems)
        beside(lambda terms: fill(k, 1, at.z, at.near, [from_second] + terms))
        give(k, 1, at.z, at.near, from_first, first_sems, at.first)

    def reduce_line(k):
        terms = [from_second, from_first]
        for d in range(depth - 1, 0, -1):

            def upward(d=d):
                z = at.z + d
                take(k, 0, z, at.own, from_second, second_sems)
                take(k, 0, z, at.own, from_first, first_sems)
                when(jnp.logical_not(at.has_below), lambda: fill(k, 0, z, at.own, terms))

                def summed():
                    take(k, 0, z, at.own, from_below, below_sems)
                    fill(k, 0, z, at.own, terms + [from_below])

                when(at.has_below, summed)
                give(k, 0, z, at.own, from_below, below_sems, at.above, lambda: at.z + d < depth)

            def downward(d=d):
                z = at.z - d
                take(k, 0, z, at.own, from_second, second_sems)
                take(k, 0, z, at.own, from_first, first_sems)
                when(jnp.logical_not(at.has_above), lambda: fill(k, 0, z, at.own, terms))

                def summed():
                    take(k, 0, z, at.own, from_above, above_sems)
                    fill(k, 0, z, at.own, terms + [from_above])

                when(at.has_above, summed)
                give(k, 0, z, at.own, from_above, above_sems, at.below, lambda: at.z >= d)

            when(at.z + d < depth, upward)
            when(at.z >= d, downward)

    def finish(k):
        for part in (1, 0):
            take(k, part, at.z, at.own, from_second, second_sems)
            take(k, part, at.z, at.own, from_first, first_sems)
        when(at.has_below, lambda: take(k, 0, at.z, at.own, from_below, below_sems))
        when(at.has_above, lambda: take(k, 0, at.z, at.own, from_above, above_sems))

        def run(terms):
            for part in range(2):
                fill(k, part, at.z, at.own, [from_second, from_first] + terms, final)

        beside(run)
        for part in range(2):
            n = lay.sizes[part] // 2
            first = 0 if part == 0 else lay.sizes[0]
            piece = pl.ds(first + (1 - core) * n, n)
            send(final.at[k, piece], twin.at[k, piece], twin_sems.at[k, part], at.sibling)

    def assemble(k):
        for part in range(2):
            n = lay.sizes[part] // 2
            first = 0 if part == 0 else lay.sizes[0]
            piece = pl.ds(first + core * n, n)
            got(twin.at[k, piece], twin_sems.at[k, part])
        for j in range(per):
            part = part_of(j)
            first = 0 if part == 0 else lay.sizes[0]
            entry = first + core * (lay.sizes[part] // 2) + offset(part, j)
            mine = pl.ds(pl.multiple_of(core * half + k * size, size), size)
            theirs = pl.ds(pl.multiple_of((1 - core) * half + k * size, size), size)
            flat[j, mine, :] = final[k, entry]
            flat[j, theirs, :] = twin[k, entry]
            out_out[j, mine, :] = final[k, entry + 1]
            out_out[j, theirs, :] = twin[k, entry + 1]

    swap = None
    gather_own(0)
    swap = load_rows()
    near_own(0)
    line(0, 1)
    line(0, 2) if depth > 2 else None
    near_line(0, 1)
    plane_own(0)
    for d in range(3, depth):
        line(0, d)
    for d in range(2, depth):
        near_line(0, d)
        plane(0, d - 1)
    plane(0, depth - 1)
    for k in range(1, SLICES):
        gather_own(k)
    for copy in local:
        copy.wait()
    for copy in swap:
        copy.wait_recv()
    scales()
    side(0)
    tables()
    for k in range(SLICES):
        more = k + 1 < SLICES
        expand(k, 0)
        if more:
            near_own(k + 1)
            line(k + 1, 1)
        expand(k, 1)
        middle(k)
        if more:
            for d in range(2, depth):
                line(k + 1, d)
            near_line(k + 1, 1)
            plane_own(k + 1)
        outer(k, 0)
        if more:
            for d in range(2, depth):
                near_line(k + 1, d)
            for d in range(1, depth):
                plane(k + 1, d)
        outer(k, 1)
        reduce_levels(k)
        reduce_second(k)
        if more:
            side(k + 1)
        else:
            for k in range(SLICES):
                reduce_first(k)
                level_sums(k)
                level_first(k)
                reduce_line(k)
                finish(k)
    for k in range(SLICES):
        assemble(k)
    for j in range(per):
        out_in[j] = flat[j].T
    for n, (like, present) in enumerate(sends):

        def sent(n=n, like=like):
            remote(like(), like(), send_sems.at[n], load_sems.at[0], at.sibling).wait_send()

        if present is None:
            sent()
        else:
            pl.when(present())(sent)


def one_section(tokens, blocks_in, blocks_out, pos_in, pos_out, cotangent):
    devices = lax.axis_size("dp")
    per = blocks_in.shape[1]
    count, width = tokens.shape
    lay = Layout(devices, per)
    depth = lay.depth
    chips = devices // 2
    size = BLOCK // 2 // SLICES
    ranks = RANK // BLOCK * size
    blocks = (width // BLOCK) * (RANK // BLOCK)
    dma = pltpu.SemaphoreType.DMA
    vmem = pltpu.VMEM
    anywhere = pl.BlockSpec(memory_space=pl.ANY)
    scalars = pl.BlockSpec(memory_space=pltpu.SMEM)
    local = pl.BlockSpec(memory_space=vmem)
    bf16, f32, i32 = jnp.bfloat16, jnp.float32, jnp.int32
    shards = (SLICES, lay.total, size, BLOCK)
    words = -(-2 * (blocks + 1) // BLOCK)
    words = -(-words // 8) * 8
    out = jax.ShapeDtypeStruct((per, BLOCK, BLOCK), bf16)
    results = pl.pallas_call(
        functools.partial(fused_kernel, devices),
        out_shape=(out, out),
        in_specs=[scalars, scalars, local, local, anywhere, anywhere],
        out_specs=(local, local),
        scratch_shapes=[
            [vmem((lay.total + 1, size, BLOCK), bf16) for _ in range(SLICES)],
            vmem((SLICES, 2 * per, size, BLOCK), bf16),
            vmem((2 * count, width), bf16),
            vmem((2 * count, width), bf16),
            vmem((2, ranks, width), bf16),
            [vmem((2 * (blocks + 1), size, BLOCK), bf16) for _ in range(SLICES)],
            vmem((2 * count, BLOCK), f32),
            vmem((devices, 8, BLOCK), i32),
            vmem((devices, BLOCK), i32),
            pltpu.SMEM((devices, BLOCK), i32),
            vmem((words, BLOCK), i32),
            pltpu.SMEM((words, BLOCK), i32),
            vmem((2, 2 * count, ranks), bf16),
            vmem(shards, bf16),
            vmem(shards, bf16),
            vmem(shards, bf16),
            vmem(shards, bf16),
            vmem(shards, bf16),
            vmem((SLICES, 4 * per, size, BLOCK), bf16),
            vmem((SLICES, 4 * per, size, BLOCK), bf16),
            vmem((per, BLOCK, BLOCK), bf16),
            dma((5,)),
            dma((400,)),
            dma((SLICES, 2)),
            dma((SLICES, 2)),
            dma((chips + 1 + chips,)),
            dma((SLICES, 2, chips)),
            dma((SLICES, depth)),
            dma((SLICES, 2, chips)),
            dma((SLICES, 2, chips)),
            dma((SLICES, 2, chips)),
            dma((SLICES, 2, chips)),
        ],
        compiler_params=pltpu.CompilerParams(
            collective_id=0, has_side_effects=True, vmem_limit_bytes=63 * 1024 * 1024
        ),
        name="fused_adapters",
    )(pos_in, pos_out, blocks_in[0], blocks_out[0], tokens, cotangent)
    return (results[0][None], results[1][None])


def solution(mesh):
    in_specs = (
        P("dp", None),
        P("section", "dp", None, None),
        P("section", "dp", None, None),
        P("section", "dp"),
        P("section", "dp"),
        P("dp", None),
    )
    out_specs = (P("section", "dp", None, None), P("section", "dp", None, None))
    body = one_section if mesh.shape["section"] == 1 else per_device
    return jax.shard_map(
        body, mesh=mesh, in_specs=in_specs, out_specs=out_specs, check_vma=False
    )
```

```python
import functools

import jax
import jax.numpy as jnp
from jax import lax
from jax.experimental import pallas as pl
from jax.experimental.pallas import tpu as pltpu
from jax.sharding import PartitionSpec as P

D = 8192
RANK = 512
BLOCK = 128
MICRO = 2


EPS = 1e-05


def from_behind(block, axis, distance):
    devices = range(lax.axis_size(axis))
    route = [(i - distance, i) for i in devices if i - distance in devices]
    return lax.ppermute(block, axis, route)


def expand(blocks, places, rows_b, cols_b):
    flat = jnp.zeros((rows_b * cols_b, BLOCK, BLOCK), blocks.dtype)
    flat = flat.at[places].set(blocks, mode="drop")
    return (
        flat.reshape(rows_b, cols_b, BLOCK, BLOCK)
        .transpose(0, 2, 1, 3)
        .reshape(rows_b * BLOCK, cols_b * BLOCK)
    )


def slot_grads(left, right, places, rows_b, cols_b):
    count = left.shape[0]
    valid = places < rows_b * cols_b
    row_block = jnp.where(valid, places // cols_b, 0).astype(jnp.int32)
    col_block = jnp.where(valid, places % cols_b, 0).astype(jnp.int32)
    left_blocks = jnp.take(left.reshape(count, rows_b, BLOCK), row_block, axis=1)
    right_blocks = jnp.take(right.reshape(count, cols_b, BLOCK), col_block, axis=1)
    result = jnp.einsum(
        "tjb,tjc->jbc", left_blocks, right_blocks, preferred_element_type=jnp.float32
    )
    return jnp.where(valid[:, None, None], result, 0.0)


def norm_parts(hidden):
    wide = hidden.astype(jnp.float32)
    scale = jnp.sqrt(jnp.mean(wide * wide, axis=-1, keepdims=True) + EPS)
    return (wide, scale)


def forward_layer(hidden, mat_a, mat_b):
    wide, scale = norm_parts(hidden)
    normed = (wide / scale).astype(jnp.bfloat16)
    pre = jnp.dot(normed, mat_a, preferred_element_type=jnp.float32)
    act = (pre * jax.nn.sigmoid(pre)).astype(jnp.bfloat16)
    return (wide + jnp.dot(act, mat_b, preferred_element_type=jnp.float32)).astype(jnp.bfloat16)


def backward_layer(hidden, upstream, mat_a, mat_b):
    wide, scale = norm_parts(hidden)
    unit = wide / scale
    normed = unit.astype(jnp.bfloat16)
    pre = jnp.dot(normed, mat_a, preferred_element_type=jnp.float32)
    sig = jax.nn.sigmoid(pre)
    act = (pre * sig).astype(jnp.bfloat16)
    dact = lax.dot_general(
        upstream, mat_b, (((1,), (1,)), ((), ())), preferred_element_type=jnp.float32
    )
    dpre = (dact * sig * (1.0 + pre * (1.0 - sig))).astype(jnp.bfloat16)
    dnorm = lax.dot_general(
        dpre, mat_a, (((1,), (1,)), ((), ())), preferred_element_type=jnp.float32
    )
    inner = jnp.mean(dnorm * unit, axis=-1, keepdims=True)
    earlier = (upstream.astype(jnp.float32) + (dnorm - unit * inner) / scale).astype(jnp.bfloat16)
    return (earlier, normed, dpre, act)


def store(stack, value, picked, active):
    updated = lax.dynamic_update_slice_in_dim(stack, value[None], picked, 0)
    return jnp.where(active, updated, stack)


def per_device(tokens, blocks_in, blocks_out, pos_in, pos_out, cotangent):
    sections = lax.axis_size("section")
    here = lax.axis_index("section")
    rows_d = D // BLOCK
    rows_k = RANK // BLOCK
    full_in, full_out, all_in, all_out = (
        lax.all_gather(blocks_in, "dp", axis=1, tiled=True),
        lax.all_gather(blocks_out, "dp", axis=1, tiled=True),
        lax.all_gather(pos_in, "dp", axis=1, tiled=True),
        lax.all_gather(pos_out, "dp", axis=1, tiled=True),
    )
    mat_a = expand(full_in[0], all_in[0], rows_d, rows_k)
    mat_b = expand(full_out[0], all_out[0], rows_k, rows_d)
    micro_rows = tokens.shape[0] // MICRO
    turns = MICRO + sections - 1
    saved = jnp.zeros((MICRO, micro_rows, D), jnp.bfloat16)
    carried = jnp.zeros((micro_rows, D), jnp.bfloat16)
    for turn in range(turns):
        micro = turn - here
        active = (micro >= 0) & (micro < MICRO)
        picked = jnp.clip(micro, 0, MICRO - 1)
        first = lax.dynamic_slice_in_dim(tokens, picked * micro_rows, micro_rows, 0)
        entering = jnp.where(here == 0, first, carried)
        saved = store(saved, entering, picked, active)
        if turn < turns - 1:
            leaving = lax.cond(
                active, lambda x: forward_layer(x, mat_a, mat_b), lambda x: x, entering
            )
            carried = from_behind(leaving, "section", 1)
    kept_normed = jnp.zeros((MICRO, micro_rows, D), jnp.bfloat16)
    kept_dpre = jnp.zeros((MICRO, micro_rows, RANK), jnp.bfloat16)
    kept_act = jnp.zeros((MICRO, micro_rows, RANK), jnp.bfloat16)
    kept_upper = jnp.zeros((MICRO, micro_rows, D), jnp.bfloat16)
    carried_grad = jnp.zeros((micro_rows, D), jnp.bfloat16)
    for turn in range(turns):
        micro = turn - (sections - 1 - here)
        active = (micro >= 0) & (micro < MICRO)
        picked = jnp.clip(micro, 0, MICRO - 1)
        last = lax.dynamic_slice_in_dim(cotangent, picked * micro_rows, micro_rows, 0)
        upstream = jnp.where(here == sections - 1, last, carried_grad)
        hidden = lax.dynamic_index_in_dim(saved, picked, 0, keepdims=False)

        def run_layer():
            return backward_layer(hidden, upstream, mat_a, mat_b)

        def skip_layer():
            return (
                upstream,
                jnp.zeros((micro_rows, D), jnp.bfloat16),
                jnp.zeros((micro_rows, RANK), jnp.bfloat16),
                jnp.zeros((micro_rows, RANK), jnp.bfloat16),
            )

        earlier, normed, dpre, act = lax.cond(active, run_layer, skip_layer)
        kept_normed = store(kept_normed, normed, picked, active)
        kept_dpre = store(kept_dpre, dpre, picked, active)
        kept_act = store(kept_act, act, picked, active)
        kept_upper = store(kept_upper, upstream, picked, active)
        if turn < turns - 1:
            carried_grad = from_behind(earlier, "section", -1)
    all_rows = MICRO * micro_rows
    terms_in = slot_grads(
        kept_normed.reshape(all_rows, D),
        kept_dpre.reshape(all_rows, RANK),
        all_in[0],
        rows_d,
        rows_k,
    )[None]
    terms_out = slot_grads(
        kept_act.reshape(all_rows, RANK),
        kept_upper.reshape(all_rows, D),
        all_out[0],
        rows_k,
        rows_d,
    )[None]
    sums_in, sums_out = (
        lax.psum_scatter(
            terms_in.astype(jnp.bfloat16), "dp", scatter_dimension=1, tiled=True
        ).astype(jnp.float32),
        lax.psum_scatter(
            terms_out.astype(jnp.bfloat16), "dp", scatter_dimension=1, tiled=True
        ).astype(jnp.float32),
    )
    return (sums_in.astype(jnp.bfloat16), sums_out.astype(jnp.bfloat16))


SLICES = 2
GATHER_PLANE = (1, 1)
REDUCE_PLANE = (1, 1)
CHUNK = 1024

def plain_order(depth):
    steps = []
    both = [d for r in range(1, depth) for d in (-r, r)]
    slices = range(SLICES)
    for k in slices:
        steps += [(name, k) for name in ("gs", "gf", "gu", "gd", "gp", "near")]
        steps += [("rows",)] if k == 0 else []
        steps += [("line", k, d) for d in both] + [("nline", k, d) for d in both]
        steps += [("pown", k)] + [("plane", k, d) for d in both] + [("side", k)]
        steps += [("tables",), ("scales",)] if k == 0 else []
        steps += [("expand", k, 0), ("expand", k, 1), ("middle", k), ("outer", k, 0), ("outer", k, 1)]
        steps += [("second", k, d, w) for d in range(depth) for w in (1, 0)]
    for k in slices:
        steps += [("lout", k, -d) for d in reversed(both)] + [("first", k, d) for d in range(depth)]
        steps += [("lsum", k), ("lfirst", k)] + [("zout", k, -d) for d in reversed(both)]
        steps += [("finish", k)]
    return steps + [("place", k) for k in slices]


ORDER = (
    ("gs", 0), ("gp", 0), ("rows",), ("gs", 1), ("gf", 0), ("gu", 0), ("gd", 1), ("gu", 1),
    ("gd", 0), ("gf", 1), ("near", 0), ("line", 0, -1), ("line", 0, 1), ("line", 0, -2),
    ("pown", 0), ("line", 0, -3), ("line", 0, 2), ("nline", 0, 1), ("nline", 0, 2),
    ("plane", 0, 1), ("nline", 0, -1), ("nline", 0, -2), ("gp", 1), ("nline", 0, -3),
    ("plane", 0, -1), ("line", 0, 3), ("near", 1), ("scales",), ("plane", 0, 2),
    ("line", 1, -1), ("nline", 0, 3), ("line", 1, 1), ("plane", 0, -2), ("nline", 1, 1),
    ("plane", 0, -3), ("side", 0), ("line", 1, 2), ("nline", 1, -1), ("plane", 0, 3),
    ("line", 1, -2), ("tables",), ("pown", 1), ("expand", 0, 0), ("line", 1, -3),
    ("line", 1, 3), ("expand", 0, 1), ("middle", 0), ("nline", 1, 3), ("nline", 1, -2),
    ("nline", 1, 2), ("plane", 1, 1), ("nline", 1, -3), ("plane", 1, -1), ("outer", 0, 0),
    ("outer", 0, 1), ("plane", 1, -2), ("plane", 1, 2), ("second", 0, 1, 1), ("lout", 0, 3),
    ("second", 0, 1, 0), ("second", 0, 3, 1), ("second", 0, 2, 0), ("lout", 0, -3),
    ("second", 0, 3, 0), ("plane", 1, -3), ("second", 0, 2, 1), ("plane", 1, 3),
    ("first", 0, 1), ("side", 1), ("lout", 0, 2), ("expand", 1, 0), ("lout", 0, -2),
    ("expand", 1, 1), ("middle", 1), ("first", 0, 3), ("zout", 0, -3), ("lout", 0, 1),
    ("outer", 1, 0), ("outer", 1, 1), ("lout", 1, 3), ("second", 1, 3, 1), ("second", 1, 1, 1),
    ("lout", 1, -3), ("first", 0, 2), ("lout", 0, -1), ("second", 1, 3, 0), ("lout", 1, 2),
    ("second", 1, 1, 0), ("second", 1, 2, 1), ("zout", 0, 3), ("first", 1, 3), ("zout", 0, -2),
    ("lout", 1, -2), ("zout", 0, 2), ("zout", 1, 3), ("first", 1, 1), ("second", 1, 2, 0),
    ("zout", 1, -3), ("lsum", 0), ("lout", 1, -1), ("lout", 1, 1), ("first", 1, 2),
    ("second", 0, 0, 1), ("second", 1, 0, 1), ("lfirst", 0), ("second", 0, 0, 0),
    ("zout", 1, -2), ("zout", 1, 2), ("first", 0, 0), ("zout", 0, -1), ("lsum", 1),
    ("zout", 0, 1), ("zout", 1, 1), ("second", 1, 0, 0), ("first", 1, 0), ("zout", 1, -1),
    ("lfirst", 1), ("finish", 0), ("place", 0), ("finish", 1), ("place", 1),
)


class Place:
    def __init__(self, devices):
        me = lax.axis_index("dp")
        self.depth = devices // 8
        self.me = me
        self.core = me % 2
        self.chip = me // 2
        x = self.chip % 2
        y = (self.chip // 2) % 2
        self.z = self.chip // 4
        dx = 1 - 2 * x
        dy = 2 * (1 - 2 * y)
        first = (1 - self.core) * dx + self.core * dy
        second = (1 - self.core) * dy + self.core * dx
        self.own = self.chip % 4
        self.near = self.own + first
        self.far = self.own + second
        self.diag = self.own + first + second
        self.sibling = me + 1 - 2 * self.core
        self.first = me + 2 * first
        self.second = me + 2 * second
        self.above = me + 8
        self.below = me - 8
        self.has_above = self.z + 1 < self.depth
        self.has_below = self.z >= 1

    def knock(self):
        barrier = pltpu.get_barrier_semaphore()

        def signal(peer):
            pl.semaphore_signal(
                barrier, inc=1, device_id={"dp": peer}, device_id_type=pl.DeviceIdType.MESH
            )

        for peer in (self.sibling, self.first, self.second):
            signal(peer)
        pl.when(self.has_above)(lambda: signal(self.above))
        pl.when(self.has_below)(lambda: signal(self.below))

        peers = 3 + self.has_above.astype(jnp.int32) + self.has_below.astype(jnp.int32)
        return lambda: pl.semaphore_wait(barrier, peers)


def remote(src, dst, send, recv, peer):
    return pltpu.make_async_remote_copy(
        src_ref=src,
        dst_ref=dst,
        send_sem=send,
        recv_sem=recv,
        device_id={"dp": peer},
        device_id_type=pl.DeviceIdType.MESH,
    )


class Layout:
    def __init__(self, devices, per, odd):
        self.split = per - odd
        self.depth = devices // 8
        self.sizes = (4 * (per - odd), 4 * odd)
        self.parts = (0, 1) if odd else (0,)
        self.plane = 16 * per
        self.total = self.depth * self.plane

    def part_of(self, j):
        return 0 if j < self.split else 1

    def first(self, part):
        return 0 if part == 0 else 2 * self.split

    def start(self, part, z, p):
        line, odd = self.sizes
        return z * self.plane + (p * line if part == 0 else 4 * line + p * odd)

    def piece(self, buf, k, part, z, p):
        span = pl.ds(self.start(part, z, p), self.sizes[part])
        return buf.at[span] if k is None else buf.at[k, span]

    def level(self, buf, k, z):
        line, odd = self.sizes
        span = pl.ds(z * self.plane + 4 * line, 4 * odd)
        return buf.at[span] if k is None else buf.at[k, span]


def fused_kernel(devices, pos_in, pos_out, own_in, own_out, tokens, cotangent, out,
                 full, stage, rows_h, rows_g, mats, grads, inverse,
                 tags, table, table_s, begin, begin_s, mid,
                 held, from_second, from_first, from_below, from_above, final, twin, flat,
                 load_sems, send_sems, pair_sems, twin_sems, tag_sems, gather_sems, level_sems,
                 second_sems, first_sems, below_sems, above_sems):
    at = Place(devices)
    depth = at.depth
    core = at.core
    per = own_in.shape[0]
    gat = [Layout(devices, per, odd) for odd in GATHER_PLANE]
    red = [Layout(devices, per, odd) for odd in REDUCE_PLANE]
    count, width = tokens.shape
    size = full[0].shape[1]
    half = BLOCK // 2
    rows_k = RANK // BLOCK
    rows_d = width // BLOCK
    blocks = rows_k * rows_d
    ranks = rows_k * size
    chunks = width // CHUNK
    sends = []
    waits = []

    def send(src, dst, recv, peer, present=None):
        remote(src, dst, send_sems.at[len(sends)], recv, peer).start()
        rows, whole = src.shape[0], src.dtype == jnp.int32
        if whole and len(src.shape) == 2:
            sends.append((lambda: tags.at[0], present))
        elif whole:
            sends.append((lambda: tags.at[pl.ds(0, rows)], present))
        else:
            sends.append((lambda: full[0].at[pl.ds(0, rows)], present))

    def got(buf, sem):
        remote(buf, buf, send_sems.at[0], sem, at.sibling).wait_recv()

    wait_peers = at.knock()

    own_rows = pl.ds(pl.multiple_of(core * count, count), count)
    local = [
        pltpu.make_async_copy(tokens, rows_h.at[own_rows], load_sems.at[0]),
        pltpu.make_async_copy(cotangent, rows_g.at[own_rows], load_sems.at[1]),
    ]
    for copy in local:
        copy.start()

    lanes = lax.broadcasted_iota(jnp.int32, tags.shape[1:], 1)
    row = jnp.full(tags.shape[1:], 2 * blocks, jnp.int32)
    for j in range(per):
        place = pos_in[0, j]
        row = jnp.where(lanes == 2 * j, jnp.where(place < blocks, place, 2 * blocks), row)
        row = jnp.where(lanes == 2 * j + 1, pos_out[0, j] + blocks, row)
    tags[at.me] = row

    for j in range(per):
        flat[0] = own_in[j].T
        flat[1] = own_out[j]
        for k in range(SLICES):
            lay = gat[k]
            part = lay.part_of(j)
            base = lay.start(part, at.z, at.own) + core * (lay.sizes[part] // 2)
            base += 2 * j - lay.first(part)
            keep = pl.ds(pl.multiple_of(core * half + k * size, size), size)
            give = pl.ds(pl.multiple_of((1 - core) * half + k * size, size), size)
            for m in range(2):
                full[k][base + m] = flat[m, keep, :]
                stage[k, 2 * j + m] = flat[m, give, :]
    for k in range(SLICES):
        full[k][gat[k].total] = jnp.zeros((size, BLOCK), jnp.bfloat16)
        grads[k][2 * blocks] = jnp.zeros((size, BLOCK), jnp.bfloat16)

    wait_peers()

    def pair(k, start):
        lay = gat[k]
        for part in lay.parts:
            n = lay.sizes[part] // 2
            base = lay.start(part, at.z, at.own) + core * n
            src, dst = stage.at[k, pl.ds(lay.first(part), n)], full[k].at[pl.ds(base, n)]
            if start:
                send(src, dst, pair_sems.at[k, part], at.sibling)
            else:
                got(src, pair_sems.at[k, part])

    send(tags.at[at.me], tags.at[at.me], tag_sems.at[2 * depth * 4], at.sibling)
    for k in range(SLICES):
        pair(k, True)

    def tag_piece(z, p):
        return tags.at[pl.ds(2 * (4 * z + p), 2)]

    def push(k, part, z, p, peer, present=None):
        if k == 0 and part == 0:
            piece = tag_piece(z, p)
            send(piece, piece, tag_sems.at[4 * z + p], peer, present)
        piece = gat[k].piece(full[k], None, part, z, p)
        send(piece, piece, gather_sems.at[k, part, 4 * z + p], peer, present)

    def arrived(k, part, z, p):
        if k == 0 and part == 0:
            got(tag_piece(z, p), tag_sems.at[4 * z + p])
        got(gat[k].piece(full[k], None, part, z, p), gather_sems.at[k, part, 4 * z + p])

    def inside(d):
        return (at.z + d < depth) if d > 0 else (at.z + d >= 0)

    def onward(d):
        return (at.has_below, at.below) if d > 0 else (at.has_above, at.above)

    def away(d):
        return (at.has_above, at.above) if d > 0 else (at.has_below, at.below)

    def own_second(k):
        pair(k, False)
        if k == 0:
            got(tags.at[at.me], tag_sems.at[2 * depth * 4])
        push(k, 0, at.z, at.own, at.second)

    def own_first(k):
        push(k, 0, at.z, at.own, at.first)

    def own_line(k, d):
        more, peer = away(d)
        pl.when(more)(lambda: push(k, 0, at.z, at.own, peer, lambda: more))

    def own_plane(k):
        for part in gat[k].parts[1:]:
            push(k, part, at.z, at.own, at.second)
            push(k, part, at.z, at.own, at.first)

    def near_own(k):
        for part in gat[k].parts:
            arrived(k, part, at.z, at.near)
            push(k, part, at.z, at.near, at.second)

    def line(k, d):
        more, peer = onward(d)
        here = inside(d)

        def run():
            z = at.z + d
            arrived(k, 0, z, at.own)
            pl.when(more)(lambda: push(k, 0, z, at.own, peer, lambda: more & here))
            push(k, 0, z, at.own, at.second, lambda: here)
            push(k, 0, z, at.own, at.first, lambda: here)

        pl.when(here)(run)

    def near_line(k, d):
        here = inside(d)

        def run():
            arrived(k, 0, at.z + d, at.near)
            push(k, 0, at.z + d, at.near, at.second, lambda: here)

        pl.when(here)(run)

    def push_level(k, z, peer, present):
        piece = gat[k].level(full[k], None, z)
        send(piece, piece, level_sems.at[k, z], peer, present)

    def plane_own(k):
        for part in gat[k].parts:
            for p in (at.far, at.diag):
                arrived(k, part, at.z, p)
        if gat[k].sizes[1]:
            for more, peer in (away(1), away(-1)):
                pl.when(more)(lambda more=more, peer=peer: push_level(k, at.z, peer, lambda: more))

    def plane(k, d):
        more, peer = onward(d)
        here = inside(d)

        def run():
            got(gat[k].level(full[k], None, at.z + d), level_sems.at[k, at.z + d])
            pl.when(more)(lambda: push_level(k, at.z + d, peer, lambda: more & here))

        if gat[k].sizes[1]:
            pl.when(here)(run)

    def side(k):
        for d in range(1 - depth, depth):

            def run(d=d):
                for p in (at.far, at.diag):
                    arrived(k, 0, at.z + d, p)

            if d:
                pl.when(inside(d))(run)

    def load_rows():
        swap = [
            remote(tokens, rows_h.at[own_rows], send_sems.at[len(sends)], load_sems.at[2], at.sibling),
            remote(cotangent, rows_g.at[own_rows], send_sems.at[len(sends) + 1], load_sems.at[3], at.sibling),
        ]
        for copy, src in zip(swap, (tokens, cotangent)):
            copy.start()
            sends.append((lambda src=src: src, None))
        waits.extend(swap)

    def scales():
        for copy in local:
            copy.wait()
        for copy in waits:
            copy.wait_recv()
        total = jnp.zeros((2 * count, BLOCK), jnp.float32)
        for i in range(0, width, BLOCK):
            wide = rows_h[:, i : i + BLOCK].astype(jnp.float32)
            total += wide * wide
        scale = jnp.sqrt(jnp.sum(total, axis=-1, keepdims=True) / width + EPS)
        inverse[...] = jnp.broadcast_to(1.0 / scale, inverse.shape)

    def tables():
        table[...] = tags[:, 0, :]
        copy = pltpu.make_async_copy(table, table_s, load_sems.at[4])
        copy.start()
        copy.wait()
        shape = begin[0].shape
        numbers = lax.broadcasted_iota(jnp.int32, shape, 0) * BLOCK
        numbers += lax.broadcasted_iota(jnp.int32, shape, 1)

        def scan(dev, found):
            z, p, which = dev // 8, (dev // 2) % 4, dev % 2
            found = list(found)
            for lane in range(2 * per):
                same = numbers == table_s[dev, lane]
                for k, lay in enumerate(gat):
                    part = lay.part_of(lane // 2)
                    entry = lay.start(part, z, p) + which * (lay.sizes[part] // 2)
                    found[k] = jnp.where(same, entry + lane - lay.first(part), found[k])
            return tuple(found)

        found = lax.fori_loop(
            0, devices, scan, tuple(jnp.full(shape, lay.total, jnp.int32) for lay in gat)
        )
        copies = []
        for k in range(SLICES):
            begin[k][...] = found[k]
            copies.append(pltpu.make_async_copy(begin[k], begin_s[k], load_sems.at[5 + k]))
            copies[k].start()
        for copy in copies:
            copy.wait()

    def expand(k, m):
        group = BLOCK // rows_k

        def step(low, carry, high):
            r = high * group + low
            into = pl.ds(pl.multiple_of(r * BLOCK, BLOCK), BLOCK)
            found = []
            for c in range(rows_k):
                if m == 0:
                    at_c = begin_s[k][high, low * rows_k + c]
                else:
                    b = blocks + c * rows_d + high * group
                    at_c = begin_s[k][b // BLOCK, b % BLOCK + low]
                found.append(full[k][at_c])
            for c in range(rows_k):
                mats[m, c * size : (c + 1) * size, into] = found[c]
            return carry

        for high in range(rows_d // group):
            lax.fori_loop(0, group, functools.partial(step, high=high), 0, unroll=4)

    def product(m):
        rows = rows_h if m == 0 else rows_g
        total = jnp.zeros((2 * count, ranks), jnp.float32)
        for i in range(0, width, CHUNK):
            total += lax.dot_general(
                rows[:, i : i + CHUNK], mats[m, :, i : i + CHUNK],
                (((1,), (1,)), ((), ())), preferred_element_type=jnp.float32,
            )
        return total

    def middle(k):
        scale = inverse[...] if ranks == BLOCK else inverse[:, :1]
        pre = product(0) * scale
        dact = product(1)
        sig = jax.nn.sigmoid(pre)
        dpre = dact * sig * (1.0 + pre * (1.0 - sig))
        mid[0] = (dpre * scale).T.astype(jnp.bfloat16)
        mid[1] = (pre * sig).T.astype(jnp.bfloat16)

    def outer(k, m):
        rows = rows_h if m == 0 else rows_g

        def step(i, carry):
            into = pl.ds(pl.multiple_of(i * CHUNK, CHUNK), CHUNK)
            part = lax.dot_general(
                mid[m], rows[:, into], (((1,), (0,)), ((), ())), preferred_element_type=jnp.float32
            ).astype(jnp.bfloat16)
            for r in range(CHUNK // BLOCK):
                col = i * (CHUNK // BLOCK) + r
                for c in range(rows_k):
                    b = col * rows_k + c if m == 0 else blocks + c * rows_d + col
                    grads[k][b] = part[c * size : (c + 1) * size, r * BLOCK : (r + 1) * BLOCK]
            return carry

        lax.fori_loop(0, chunks, step, 0)

    def fill(k, part, z, p, terms, into=None):
        lay = red[k]
        n = lay.sizes[part] // 2
        first = lay.first(part)
        base = lay.start(part, z, p)

        def step(which, carry):
            dev = 2 * (4 * z + p) + which
            for i in range(n):
                entry = base + which * n + i
                value = grads[k][table_s[dev, first + i]]
                if terms:
                    value = value.astype(jnp.float32)
                    for term in terms:
                        value += term[k, entry].astype(jnp.float32)
                    value = value.astype(jnp.bfloat16)
                if into is None:
                    held[k, entry] = value
                else:
                    into[k, 2 * first + which * n + i] = value
            return carry

        lax.fori_loop(0, 2, step, 0)

    def give(k, part, z, p, buf, sems, peer, present=None):
        src = red[k].piece(held, k, part, z, p)
        send(src, red[k].piece(buf, k, part, z, p), sems.at[k, part, 4 * z + p], peer, present)

    def take(k, part, z, p, buf, sems):
        got(red[k].piece(buf, k, part, z, p), sems.at[k, part, 4 * z + p])

    def behind(d):
        if d > 0:
            return at.has_below, from_below, below_sems, at.above
        return at.has_above, from_above, above_sems, at.below

    def level_out(k, d):
        before, buf, sems, peer = behind(d)
        here = inside(d)

        def run():
            z = at.z + d

            def fills(terms):
                for p in range(4):
                    fill(k, 1, z, p, terms)

            def summed():
                got(red[k].level(buf, k, z), sems.at[k, 1, z])
                fills([buf])

            pl.when(jnp.logical_not(before))(lambda: fills([]))
            pl.when(before)(summed)
            send(
                red[k].level(held, k, z), red[k].level(buf, k, z), sems.at[k, 1, z],
                peer, lambda: here,
            )

        if red[k].sizes[1]:
            pl.when(here)(run)

    def beside(run):
        above, below = at.has_above, at.has_below
        pl.when(below & above)(lambda: run([from_below, from_above]))
        pl.when(below & jnp.logical_not(above))(lambda: run([from_below]))
        pl.when(above & jnp.logical_not(below))(lambda: run([from_above]))

    def second(k, d, which):
        z = (at.z + d) % depth
        p = at.diag if which else at.far
        fill(k, 0, z, p, [])
        give(k, 0, z, p, from_second, second_sems, at.second)

    def first(k, d):
        z = (at.z + d) % depth
        take(k, 0, z, at.near, from_second, second_sems)
        fill(k, 0, z, at.near, [from_second])
        give(k, 0, z, at.near, from_first, first_sems, at.first)

    def level_sums(k):
        if not red[k].sizes[1]:
            return
        for more, buf, sems in (
            (at.has_below, from_below, below_sems), (at.has_above, from_above, above_sems)
        ):
            pl.when(more)(
                lambda buf=buf, sems=sems: got(red[k].level(buf, k, at.z), sems.at[k, 1, at.z])
            )

        def run(terms):
            for p in (at.diag, at.far):
                fill(k, 1, at.z, p, terms)

        beside(run)
        for p in (at.diag, at.far):
            give(k, 1, at.z, p, from_second, second_sems, at.second)

    def level_first(k):
        if not red[k].sizes[1]:
            return
        take(k, 1, at.z, at.near, from_second, second_sems)
        beside(lambda terms: fill(k, 1, at.z, at.near, [from_second] + terms))
        give(k, 1, at.z, at.near, from_first, first_sems, at.first)

    def line_out(k, d):
        before, buf, sems, peer = behind(d)
        here = inside(d)
        terms = [from_second, from_first]

        def run():
            z = at.z + d
            take(k, 0, z, at.own, from_second, second_sems)
            take(k, 0, z, at.own, from_first, first_sems)

            def summed():
                take(k, 0, z, at.own, buf, sems)
                fill(k, 0, z, at.own, terms + [buf])

            pl.when(jnp.logical_not(before))(lambda: fill(k, 0, z, at.own, terms))
            pl.when(before)(summed)
            give(k, 0, z, at.own, buf, sems, peer, lambda: here)

        pl.when(here)(run)

    def finish(k):
        lay = red[k]
        for part in lay.parts[::-1]:
            take(k, part, at.z, at.own, from_second, second_sems)
            take(k, part, at.z, at.own, from_first, first_sems)
        pl.when(at.has_below)(lambda: take(k, 0, at.z, at.own, from_below, below_sems))
        pl.when(at.has_above)(lambda: take(k, 0, at.z, at.own, from_above, above_sems))

        def run(terms):
            for part in lay.parts:
                fill(k, part, at.z, at.own, [from_second, from_first] + terms, final)

        beside(run)
        for part in lay.parts:
            n = lay.sizes[part] // 2
            piece = pl.ds(2 * lay.first(part) + (1 - core) * n, n)
            send(final.at[k, piece], twin.at[k, piece], twin_sems.at[k, part], at.sibling)

    def assemble(k):
        lay = red[k]
        for part in lay.parts:
            n = lay.sizes[part] // 2
            piece = pl.ds(2 * lay.first(part) + core * n, n)
            got(twin.at[k, piece], twin_sems.at[k, part])
        mine = pl.ds(pl.multiple_of(core * half + k * size, size), size)
        theirs = pl.ds(pl.multiple_of((1 - core) * half + k * size, size), size)
        for j in range(per):
            part = lay.part_of(j)
            entry = lay.first(part) + core * (lay.sizes[part] // 2) + 2 * j
            flat[j, mine, :] = final[k, entry]
            flat[j, theirs, :] = twin[k, entry]
            out[1, j, mine, :] = final[k, entry + 1]
            out[1, j, theirs, :] = twin[k, entry + 1]

    steps = {
        "gs": own_second, "gf": own_first, "gu": lambda k: own_line(k, 1),
        "gd": lambda k: own_line(k, -1), "gp": own_plane, "rows": load_rows,
        "near": near_own, "line": line, "nline": near_line, "pown": plane_own, "plane": plane,
        "side": side, "tables": tables, "scales": scales, "expand": expand, "middle": middle,
        "outer": outer, "lout": level_out, "second": second, "first": first,
        "lsum": level_sums, "lfirst": level_first, "zout": line_out, "finish": finish,
        "place": assemble,
    }
    for step in ORDER if depth == 4 and SLICES == 2 else plain_order(depth):
        steps[step[0]](*step[1:])
    for j in range(per):
        out[0, j] = flat[j].T
    for n, (like, present) in enumerate(sends):

        def sent(n=n, like=like):
            remote(like(), like(), send_sems.at[n], load_sems.at[0], at.sibling).wait_send()

        if present is None:
            sent()
        else:
            pl.when(present())(sent)


def one_section(tokens, blocks_in, blocks_out, pos_in, pos_out, cotangent):
    devices = lax.axis_size("dp")
    per = blocks_in.shape[1]
    count, width = tokens.shape
    depth = devices // 8
    chips = devices // 2
    entries = 4 * per * chips
    size = BLOCK // 2 // SLICES
    ranks = RANK // BLOCK * size
    blocks = (width // BLOCK) * (RANK // BLOCK)
    dma = pltpu.SemaphoreType.DMA
    vmem = pltpu.VMEM
    anywhere = pl.BlockSpec(memory_space=pl.ANY)
    scalars = pl.BlockSpec(memory_space=pltpu.SMEM)
    local = pl.BlockSpec(memory_space=vmem)
    bf16, f32, i32 = jnp.bfloat16, jnp.float32, jnp.int32
    shards = (SLICES, entries, size, BLOCK)
    words = -(-(2 * blocks + 1) // BLOCK)
    words = -(-words // 8) * 8
    results = pl.pallas_call(
        functools.partial(fused_kernel, devices),
        out_shape=jax.ShapeDtypeStruct((2, per, BLOCK, BLOCK), bf16),
        in_specs=[scalars, scalars, local, local, anywhere, anywhere],
        out_specs=local,
        scratch_shapes=[
            [vmem((entries + 1, size, BLOCK), bf16) for _ in range(SLICES)],
            vmem((SLICES, 2 * per, size, BLOCK), bf16),
            vmem((2 * count, width), bf16),
            vmem((2 * count, width), bf16),
            vmem((2, ranks, width), bf16),
            [vmem((2 * blocks + 1, size, BLOCK), bf16) for _ in range(SLICES)],
            vmem((2 * count, BLOCK), f32),
            vmem((devices, 8, BLOCK), i32),
            vmem((devices, BLOCK), i32),
            pltpu.SMEM((devices, BLOCK), i32),
            [vmem((words, BLOCK), i32) for _ in range(SLICES)],
            [pltpu.SMEM((words, BLOCK), i32) for _ in range(SLICES)],
            vmem((2, ranks, 2 * count), bf16),
            vmem(shards, bf16),
            vmem(shards, bf16),
            vmem(shards, bf16),
            vmem(shards, bf16),
            vmem(shards, bf16),
            vmem((SLICES, 4 * per, size, BLOCK), bf16),
            vmem((SLICES, 4 * per, size, BLOCK), bf16),
            vmem((per, BLOCK, BLOCK), bf16),
            dma((5 + SLICES,)),
            dma((400,)),
            dma((SLICES, 2)),
            dma((SLICES, 2)),
            dma((chips + 1 + chips,)),
            dma((SLICES, 2, chips)),
            dma((SLICES, depth)),
            dma((SLICES, 2, chips)),
            dma((SLICES, 2, chips)),
            dma((SLICES, 2, chips)),
            dma((SLICES, 2, chips)),
        ],
        compiler_params=pltpu.CompilerParams(
            collective_id=0, has_side_effects=True, vmem_limit_bytes=63 * 1024 * 1024
        ),
        name="fused_adapters",
    )(pos_in, pos_out, blocks_in[0], blocks_out[0], tokens, cotangent)
    return (results[0][None], results[1][None])


def solution(mesh):
    in_specs = (
        P("dp", None),
        P("section", "dp", None, None),
        P("section", "dp", None, None),
        P("section", "dp"),
        P("section", "dp"),
        P("dp", None),
    )
    out_specs = (P("section", "dp", None, None), P("section", "dp", None, None))
    body = one_section if mesh.shape["section"] == 1 else per_device
    return jax.shard_map(
        body, mesh=mesh, in_specs=in_specs, out_specs=out_specs, check_vma=False
    )
```

```python
import functools

import jax
import jax.numpy as jnp
from jax import lax
from jax.experimental import pallas as pl
from jax.experimental.pallas import tpu as pltpu
from jax.sharding import PartitionSpec as P

D = 8192
RANK = 512
BLOCK = 128
MICRO = 2


EPS = 1e-05


def from_behind(block, axis, distance):
    devices = range(lax.axis_size(axis))
    route = [(i - distance, i) for i in devices if i - distance in devices]
    return lax.ppermute(block, axis, route)


def expand(blocks, places, rows_b, cols_b):
    flat = jnp.zeros((rows_b * cols_b, BLOCK, BLOCK), blocks.dtype)
    flat = flat.at[places].set(blocks, mode="drop")
    return (
        flat.reshape(rows_b, cols_b, BLOCK, BLOCK)
        .transpose(0, 2, 1, 3)
        .reshape(rows_b * BLOCK, cols_b * BLOCK)
    )


def slot_grads(left, right, places, rows_b, cols_b):
    count = left.shape[0]
    valid = places < rows_b * cols_b
    row_block = jnp.where(valid, places // cols_b, 0).astype(jnp.int32)
    col_block = jnp.where(valid, places % cols_b, 0).astype(jnp.int32)
    left_blocks = jnp.take(left.reshape(count, rows_b, BLOCK), row_block, axis=1)
    right_blocks = jnp.take(right.reshape(count, cols_b, BLOCK), col_block, axis=1)
    result = jnp.einsum(
        "tjb,tjc->jbc", left_blocks, right_blocks, preferred_element_type=jnp.float32
    )
    return jnp.where(valid[:, None, None], result, 0.0)


def norm_parts(hidden):
    wide = hidden.astype(jnp.float32)
    scale = jnp.sqrt(jnp.mean(wide * wide, axis=-1, keepdims=True) + EPS)
    return (wide, scale)


def forward_layer(hidden, mat_a, mat_b):
    wide, scale = norm_parts(hidden)
    normed = (wide / scale).astype(jnp.bfloat16)
    pre = jnp.dot(normed, mat_a, preferred_element_type=jnp.float32)
    act = (pre * jax.nn.sigmoid(pre)).astype(jnp.bfloat16)
    return (wide + jnp.dot(act, mat_b, preferred_element_type=jnp.float32)).astype(jnp.bfloat16)


def backward_layer(hidden, upstream, mat_a, mat_b):
    wide, scale = norm_parts(hidden)
    unit = wide / scale
    normed = unit.astype(jnp.bfloat16)
    pre = jnp.dot(normed, mat_a, preferred_element_type=jnp.float32)
    sig = jax.nn.sigmoid(pre)
    act = (pre * sig).astype(jnp.bfloat16)
    dact = lax.dot_general(
        upstream, mat_b, (((1,), (1,)), ((), ())), preferred_element_type=jnp.float32
    )
    dpre = (dact * sig * (1.0 + pre * (1.0 - sig))).astype(jnp.bfloat16)
    dnorm = lax.dot_general(
        dpre, mat_a, (((1,), (1,)), ((), ())), preferred_element_type=jnp.float32
    )
    inner = jnp.mean(dnorm * unit, axis=-1, keepdims=True)
    earlier = (upstream.astype(jnp.float32) + (dnorm - unit * inner) / scale).astype(jnp.bfloat16)
    return (earlier, normed, dpre, act)


def store(stack, value, picked, active):
    updated = lax.dynamic_update_slice_in_dim(stack, value[None], picked, 0)
    return jnp.where(active, updated, stack)


def per_device(tokens, blocks_in, blocks_out, pos_in, pos_out, cotangent):
    sections = lax.axis_size("section")
    here = lax.axis_index("section")
    rows_d = D // BLOCK
    rows_k = RANK // BLOCK
    full_in, full_out, all_in, all_out = (
        lax.all_gather(blocks_in, "dp", axis=1, tiled=True),
        lax.all_gather(blocks_out, "dp", axis=1, tiled=True),
        lax.all_gather(pos_in, "dp", axis=1, tiled=True),
        lax.all_gather(pos_out, "dp", axis=1, tiled=True),
    )
    mat_a = expand(full_in[0], all_in[0], rows_d, rows_k)
    mat_b = expand(full_out[0], all_out[0], rows_k, rows_d)
    micro_rows = tokens.shape[0] // MICRO
    turns = MICRO + sections - 1
    saved = jnp.zeros((MICRO, micro_rows, D), jnp.bfloat16)
    carried = jnp.zeros((micro_rows, D), jnp.bfloat16)
    for turn in range(turns):
        micro = turn - here
        active = (micro >= 0) & (micro < MICRO)
        picked = jnp.clip(micro, 0, MICRO - 1)
        first = lax.dynamic_slice_in_dim(tokens, picked * micro_rows, micro_rows, 0)
        entering = jnp.where(here == 0, first, carried)
        saved = store(saved, entering, picked, active)
        if turn < turns - 1:
            leaving = lax.cond(
                active, lambda x: forward_layer(x, mat_a, mat_b), lambda x: x, entering
            )
            carried = from_behind(leaving, "section", 1)
    kept_normed = jnp.zeros((MICRO, micro_rows, D), jnp.bfloat16)
    kept_dpre = jnp.zeros((MICRO, micro_rows, RANK), jnp.bfloat16)
    kept_act = jnp.zeros((MICRO, micro_rows, RANK), jnp.bfloat16)
    kept_upper = jnp.zeros((MICRO, micro_rows, D), jnp.bfloat16)
    carried_grad = jnp.zeros((micro_rows, D), jnp.bfloat16)
    for turn in range(turns):
        micro = turn - (sections - 1 - here)
        active = (micro >= 0) & (micro < MICRO)
        picked = jnp.clip(micro, 0, MICRO - 1)
        last = lax.dynamic_slice_in_dim(cotangent, picked * micro_rows, micro_rows, 0)
        upstream = jnp.where(here == sections - 1, last, carried_grad)
        hidden = lax.dynamic_index_in_dim(saved, picked, 0, keepdims=False)

        def run_layer():
            return backward_layer(hidden, upstream, mat_a, mat_b)

        def skip_layer():
            return (
                upstream,
                jnp.zeros((micro_rows, D), jnp.bfloat16),
                jnp.zeros((micro_rows, RANK), jnp.bfloat16),
                jnp.zeros((micro_rows, RANK), jnp.bfloat16),
            )

        earlier, normed, dpre, act = lax.cond(active, run_layer, skip_layer)
        kept_normed = store(kept_normed, normed, picked, active)
        kept_dpre = store(kept_dpre, dpre, picked, active)
        kept_act = store(kept_act, act, picked, active)
        kept_upper = store(kept_upper, upstream, picked, active)
        if turn < turns - 1:
            carried_grad = from_behind(earlier, "section", -1)
    all_rows = MICRO * micro_rows
    terms_in = slot_grads(
        kept_normed.reshape(all_rows, D),
        kept_dpre.reshape(all_rows, RANK),
        all_in[0],
        rows_d,
        rows_k,
    )[None]
    terms_out = slot_grads(
        kept_act.reshape(all_rows, RANK),
        kept_upper.reshape(all_rows, D),
        all_out[0],
        rows_k,
        rows_d,
    )[None]
    sums_in, sums_out = (
        lax.psum_scatter(
            terms_in.astype(jnp.bfloat16), "dp", scatter_dimension=1, tiled=True
        ).astype(jnp.float32),
        lax.psum_scatter(
            terms_out.astype(jnp.bfloat16), "dp", scatter_dimension=1, tiled=True
        ).astype(jnp.float32),
    )
    return (sums_in.astype(jnp.bfloat16), sums_out.astype(jnp.bfloat16))


SLICES = 2
GATHER_PLANE = (1, 1)
REDUCE_PLANE = (1, 1)
CHUNK = 1024

def plain_order(depth):
    steps = []
    both = [d for r in range(1, depth) for d in (-r, r)]
    slices = range(SLICES)
    for k in slices:
        steps += [(name, k) for name in ("gs", "gf", "gu", "gd", "gp", "near")]
        steps += [("rows",)] if k == 0 else []
        steps += [("line", k, d) for d in both] + [("nline", k, d) for d in both]
        steps += [("pown", k)] + [("plane", k, d) for d in both] + [("side", k)]
        steps += [("tables",), ("scales",)] if k == 0 else []
        steps += [("expand", k, 0), ("expand", k, 1), ("middle", k), ("outer", k, 0), ("outer", k, 1)]
        steps += [("second", k, d, w) for d in range(depth) for w in (1, 0)]
    for k in slices:
        steps += [("lout", k, -d) for d in reversed(both)] + [("first", k, d) for d in range(depth)]
        steps += [("lsum", k), ("lfirst", k)] + [("zout", k, -d) for d in reversed(both)]
        steps += [("finish", k)]
    return steps + [("place", k) for k in slices]


ORDER = (
    ("gs", 0), ("gu", 0), ("gf", 0), ("gp", 0), ("rows",), ("gs", 1), ("gd", 0), ("near", 0),
    ("line", 0, 1), ("gd", 1), ("line", 0, -1), ("line", 0, -2), ("line", 0, 2), ("pown", 0),
    ("gf", 1), ("nline", 0, 1), ("line", 0, -3), ("nline", 0, -1), ("nline", 0, -3),
    ("line", 0, 3), ("nline", 0, 2), ("plane", 0, 1), ("plane", 0, -1), ("gu", 1), ("scales",),
    ("nline", 0, 3), ("plane", 0, 2), ("plane", 0, -2), ("nline", 0, -2), ("gp", 1),
    ("near", 1), ("line", 1, -1), ("plane", 0, 3), ("plane", 0, -3), ("line", 1, 1),
    ("side", 0), ("tables",), ("line", 1, -2), ("line", 1, 2), ("expand", 0, 0), ("pown", 1),
    ("expand", 0, 1), ("nline", 1, 1), ("nline", 1, -1), ("line", 1, -3), ("line", 1, 3),
    ("middle", 0), ("plane", 1, -1), ("plane", 1, 1), ("nline", 1, 2), ("nline", 1, -2),
    ("outer", 0, 0), ("nline", 1, 3), ("nline", 1, -3), ("plane", 1, -2), ("outer", 0, 1),
    ("plane", 1, 2), ("second", 0, 3, 1), ("lout", 0, 3), ("lout", 0, -3), ("second", 0, 2, 1),
    ("second", 0, 1, 1), ("side", 1), ("second", 0, 3, 0), ("second", 0, 1, 0),
    ("second", 0, 2, 0), ("plane", 1, 3), ("plane", 1, -3), ("expand", 1, 0), ("lout", 0, 2),
    ("expand", 1, 1), ("lout", 0, -2), ("first", 0, 3), ("middle", 1), ("first", 0, 2),
    ("lout", 0, 1), ("first", 0, 1), ("lout", 0, -1), ("outer", 1, 0), ("zout", 0, 3),
    ("outer", 1, 1), ("second", 1, 3, 1), ("lout", 1, 3), ("second", 1, 1, 1), ("zout", 0, 2),
    ("lout", 1, -3), ("second", 1, 2, 1), ("zout", 0, -3), ("lout", 1, -2), ("first", 1, 3),
    ("second", 1, 1, 0), ("second", 1, 3, 0), ("second", 1, 2, 0), ("first", 1, 1), ("lsum", 0),
    ("lout", 1, 2), ("lout", 1, -1), ("second", 1, 0, 1), ("second", 0, 0, 1), ("lout", 1, 1),
    ("zout", 1, -3), ("zout", 1, 3), ("zout", 0, 1), ("zout", 0, -2), ("first", 1, 2),
    ("lsum", 1), ("zout", 1, -2), ("lfirst", 0), ("second", 0, 0, 0), ("zout", 1, 2),
    ("first", 1, 0), ("zout", 0, -1), ("second", 1, 0, 0), ("first", 0, 0), ("zout", 1, -1),
    ("zout", 1, 1), ("lfirst", 1), ("finish", 0), ("finish", 1), ("place", 0), ("place", 1),
)


class Place:
    def __init__(self, devices):
        me = lax.axis_index("dp")
        self.depth = devices // 8
        self.me = me
        self.core = me % 2
        self.chip = me // 2
        x = self.chip % 2
        y = (self.chip // 2) % 2
        self.z = self.chip // 4
        dx = 1 - 2 * x
        dy = 2 * (1 - 2 * y)
        first = (1 - self.core) * dx + self.core * dy
        second = (1 - self.core) * dy + self.core * dx
        self.own = self.chip % 4
        self.near = self.own + first
        self.far = self.own + second
        self.diag = self.own + first + second
        self.sibling = me + 1 - 2 * self.core
        self.first = me + 2 * first
        self.second = me + 2 * second
        self.above = me + 8
        self.below = me - 8
        self.has_above = self.z + 1 < self.depth
        self.has_below = self.z >= 1

    def knock(self):
        barrier = pltpu.get_barrier_semaphore()

        def signal(peer):
            pl.semaphore_signal(
                barrier, inc=1, device_id={"dp": peer}, device_id_type=pl.DeviceIdType.MESH
            )

        for peer in (self.sibling, self.first, self.second):
            signal(peer)
        pl.when(self.has_above)(lambda: signal(self.above))
        pl.when(self.has_below)(lambda: signal(self.below))

        peers = 3 + self.has_above.astype(jnp.int32) + self.has_below.astype(jnp.int32)
        return lambda: pl.semaphore_wait(barrier, peers)


def remote(src, dst, send, recv, peer):
    return pltpu.make_async_remote_copy(
        src_ref=src,
        dst_ref=dst,
        send_sem=send,
        recv_sem=recv,
        device_id={"dp": peer},
        device_id_type=pl.DeviceIdType.MESH,
    )


class Layout:
    def __init__(self, devices, per, odd):
        self.split = per - odd
        self.depth = devices // 8
        self.sizes = (4 * (per - odd), 4 * odd)
        self.parts = (0, 1) if odd else (0,)
        self.plane = 16 * per
        self.total = self.depth * self.plane

    def part_of(self, j):
        return 0 if j < self.split else 1

    def first(self, part):
        return 0 if part == 0 else 2 * self.split

    def start(self, part, z, p):
        line, odd = self.sizes
        return z * self.plane + (p * line if part == 0 else 4 * line + p * odd)

    def piece(self, buf, k, part, z, p):
        span = pl.ds(self.start(part, z, p), self.sizes[part])
        return buf.at[span] if k is None else buf.at[k, span]

    def level(self, buf, k, z):
        line, odd = self.sizes
        span = pl.ds(z * self.plane + 4 * line, 4 * odd)
        return buf.at[span] if k is None else buf.at[k, span]


def fused_kernel(devices, pos_in, pos_out, blocks_in, blocks_out, tokens, cotangent, out,
                 own, full, stage, rows_h, rows_g, mats, grads, inverse,
                 tags, table, table_s, begin, begin_s, mid,
                 held, from_second, from_first, from_below, from_above, final, twin, flat,
                 load_sems, send_sems, pair_sems, twin_sems, tag_sems, gather_sems, level_sems,
                 second_sems, first_sems, below_sems, above_sems):
    at = Place(devices)
    depth = at.depth
    core = at.core
    per = blocks_in.shape[0]
    gat = [Layout(devices, per, odd) for odd in GATHER_PLANE]
    red = [Layout(devices, per, odd) for odd in REDUCE_PLANE]
    count, width = tokens.shape
    size = full[0].shape[1]
    half = BLOCK // 2
    rows_k = RANK // BLOCK
    rows_d = width // BLOCK
    blocks = rows_k * rows_d
    ranks = rows_k * size
    chunks = width // CHUNK
    sends = []
    waits = []

    def send(src, dst, recv, peer, present=None):
        remote(src, dst, send_sems.at[len(sends)], recv, peer).start()
        rows, whole = src.shape[0], src.dtype == jnp.int32
        if whole and len(src.shape) == 2:
            sends.append((lambda: tags.at[0], present))
        elif whole:
            sends.append((lambda: tags.at[pl.ds(0, rows)], present))
        else:
            sends.append((lambda: full[0].at[pl.ds(0, rows)], present))

    def got(buf, sem):
        remote(buf, buf, send_sems.at[0], sem, at.sibling).wait_recv()

    wait_peers = at.knock()
    own_loads = [
        pltpu.make_async_copy(blocks_in, own.at[0], load_sems.at[5]),
        pltpu.make_async_copy(blocks_out, own.at[1], load_sems.at[6]),
    ]
    for copy in own_loads:
        copy.start()

    own_rows = pl.ds(pl.multiple_of(core * count, count), count)
    local = [
        pltpu.make_async_copy(tokens, rows_h.at[own_rows], load_sems.at[0]),
        pltpu.make_async_copy(cotangent, rows_g.at[own_rows], load_sems.at[1]),
    ]
    for copy in local:
        copy.start()

    lanes = lax.broadcasted_iota(jnp.int32, tags.shape[1:], 1)
    row = jnp.full(tags.shape[1:], 2 * blocks, jnp.int32)
    for j in range(per):
        place = pos_in[0, j]
        row = jnp.where(lanes == 2 * j, jnp.where(place < blocks, place, 2 * blocks), row)
        row = jnp.where(lanes == 2 * j + 1, pos_out[0, j] + blocks, row)
    tags[at.me] = row

    for copy in own_loads:
        copy.wait()
    for j in range(per):
        flat[0] = own[0, j].T
        flat[1] = own[1, j]
        for k in range(SLICES):
            lay = gat[k]
            part = lay.part_of(j)
            base = lay.start(part, at.z, at.own) + core * (lay.sizes[part] // 2)
            base += 2 * j - lay.first(part)
            keep = pl.ds(pl.multiple_of(core * half + k * size, size), size)
            give = pl.ds(pl.multiple_of((1 - core) * half + k * size, size), size)
            for m in range(2):
                full[k][base + m] = flat[m, keep, :]
                stage[k, 2 * j + m] = flat[m, give, :]
    for k in range(SLICES):
        full[k][gat[k].total] = jnp.zeros((size, BLOCK), jnp.bfloat16)
        grads[k][2 * blocks] = jnp.zeros((size, BLOCK), jnp.bfloat16)

    wait_peers()

    def pair(k, start):
        lay = gat[k]
        for part in lay.parts:
            n = lay.sizes[part] // 2
            base = lay.start(part, at.z, at.own) + core * n
            src, dst = stage.at[k, pl.ds(lay.first(part), n)], full[k].at[pl.ds(base, n)]
            if start:
                send(src, dst, pair_sems.at[k, part], at.sibling)
            else:
                got(src, pair_sems.at[k, part])

    send(tags.at[at.me], tags.at[at.me], tag_sems.at[4 * depth], at.sibling)
    for k in range(SLICES):
        pair(k, True)

    def tag_piece(z, p):
        return tags.at[pl.ds(2 * (4 * z + p), 2)]

    def push(k, part, z, p, peer, present=None):
        if k == 0 and part == 0:
            piece = tag_piece(z, p)
            send(piece, piece, tag_sems.at[4 * z + p], peer, present)
        piece = gat[k].piece(full[k], None, part, z, p)
        send(piece, piece, gather_sems.at[k, 4 * z + p if part == 0 else 4 * depth + p], peer, present)

    def arrived(k, part, z, p):
        if k == 0 and part == 0:
            got(tag_piece(z, p), tag_sems.at[4 * z + p])
        got(gat[k].piece(full[k], None, part, z, p), gather_sems.at[k, 4 * z + p if part == 0 else 4 * depth + p])

    def inside(d):
        return (at.z + d < depth) if d > 0 else (at.z + d >= 0)

    def onward(d):
        return (at.has_below, at.below) if d > 0 else (at.has_above, at.above)

    def away(d):
        return (at.has_above, at.above) if d > 0 else (at.has_below, at.below)

    def own_second(k):
        pair(k, False)
        if k == 0:
            got(tags.at[at.me], tag_sems.at[4 * depth])
        push(k, 0, at.z, at.own, at.second)

    def own_first(k):
        push(k, 0, at.z, at.own, at.first)

    def own_line(k, d):
        more, peer = away(d)
        pl.when(more)(lambda: push(k, 0, at.z, at.own, peer, lambda: more))

    def own_plane(k):
        for part in gat[k].parts[1:]:
            push(k, part, at.z, at.own, at.second)
            push(k, part, at.z, at.own, at.first)

    def near_own(k):
        for part in gat[k].parts:
            arrived(k, part, at.z, at.near)
            push(k, part, at.z, at.near, at.second)

    def line(k, d):
        more, peer = onward(d)
        here = inside(d)

        def run():
            z = at.z + d
            arrived(k, 0, z, at.own)
            pl.when(more)(lambda: push(k, 0, z, at.own, peer, lambda: more & here))
            push(k, 0, z, at.own, at.second, lambda: here)
            push(k, 0, z, at.own, at.first, lambda: here)

        pl.when(here)(run)

    def near_line(k, d):
        here = inside(d)

        def run():
            arrived(k, 0, at.z + d, at.near)
            push(k, 0, at.z + d, at.near, at.second, lambda: here)

        pl.when(here)(run)

    def push_level(k, z, peer, present):
        piece = gat[k].level(full[k], None, z)
        send(piece, piece, level_sems.at[k, z], peer, present)

    def plane_own(k):
        for part in gat[k].parts:
            for p in (at.far, at.diag):
                arrived(k, part, at.z, p)
        if gat[k].sizes[1]:
            for more, peer in (away(1), away(-1)):
                pl.when(more)(lambda more=more, peer=peer: push_level(k, at.z, peer, lambda: more))

    def plane(k, d):
        more, peer = onward(d)
        here = inside(d)

        def run():
            got(gat[k].level(full[k], None, at.z + d), level_sems.at[k, at.z + d])
            pl.when(more)(lambda: push_level(k, at.z + d, peer, lambda: more & here))

        if gat[k].sizes[1]:
            pl.when(here)(run)

    def side(k):
        for d in range(1 - depth, depth):

            def run(d=d):
                for p in (at.far, at.diag):
                    arrived(k, 0, at.z + d, p)

            if d:
                pl.when(inside(d))(run)

    def load_rows():
        swap = [
            remote(tokens, rows_h.at[own_rows], send_sems.at[len(sends)], load_sems.at[2], at.sibling),
            remote(cotangent, rows_g.at[own_rows], send_sems.at[len(sends) + 1], load_sems.at[3], at.sibling),
        ]
        for copy, src in zip(swap, (tokens, cotangent)):
            copy.start()
            sends.append((lambda src=src: src, None))
        waits.extend(swap)

    def scales():
        for copy in local:
            copy.wait()
        for copy in waits:
            copy.wait_recv()
        total = jnp.zeros((2 * count, BLOCK), jnp.float32)
        for i in range(0, width, BLOCK):
            wide = rows_h[:, i : i + BLOCK].astype(jnp.float32)
            total += wide * wide
        scale = jnp.sqrt(jnp.sum(total, axis=-1, keepdims=True) / width + EPS)
        inverse[...] = jnp.broadcast_to(1.0 / scale, inverse.shape)

    def tables():
        table[...] = tags[:, 0, :]
        copy = pltpu.make_async_copy(table, table_s, load_sems.at[4])
        copy.start()
        copy.wait()
        shape = begin[0].shape
        numbers = lax.broadcasted_iota(jnp.int32, shape, 0) * BLOCK
        numbers += lax.broadcasted_iota(jnp.int32, shape, 1)

        kinds = {lay.split: lay for lay in gat}

        def scan(dev, found):
            z, p, which = dev // 8, (dev // 2) % 4, dev % 2
            bases = [
                [lay.start(part, z, p) + which * (lay.sizes[part] // 2) for part in range(2)]
                for lay in kinds.values()
            ]
            found = list(found)
            for lane in range(2 * per):
                same = numbers == table_s[dev, lane]
                for n, lay in enumerate(kinds.values()):
                    part = lay.part_of(lane // 2)
                    entry = bases[n][part] + (lane - lay.first(part))
                    found[n] = jnp.where(same, entry, found[n])
            return tuple(found)

        found = lax.fori_loop(
            0, devices, scan,
            tuple(jnp.full(shape, lay.total, jnp.int32) for lay in kinds.values()),
        )
        found = dict(zip(kinds, found))
        copies = []
        for k in range(SLICES):
            begin[k][...] = found[gat[k].split]
            copies.append(pltpu.make_async_copy(begin[k], begin_s[k], load_sems.at[7 + k]))
            copies[k].start()
        for copy in copies:
            copy.wait()

    def expand(k, m):
        group = BLOCK // rows_k

        def step(low, carry, high):
            r = high * group + low
            into = pl.ds(pl.multiple_of(r * BLOCK, BLOCK), BLOCK)
            found = []
            for c in range(rows_k):
                if m == 0:
                    at_c = begin_s[k][high, low * rows_k + c]
                else:
                    b = blocks + c * rows_d + high * group
                    at_c = begin_s[k][b // BLOCK, b % BLOCK + low]
                found.append(full[k][at_c])
            for c in range(rows_k):
                mats[m, c * size : (c + 1) * size, into] = found[c]
            return carry

        for high in range(rows_d // group):
            lax.fori_loop(0, group, functools.partial(step, high=high), 0, unroll=4)

    def product(m):
        rows = rows_h if m == 0 else rows_g
        total = jnp.zeros((2 * count, ranks), jnp.float32)
        for i in range(0, width, CHUNK):
            total += lax.dot_general(
                rows[:, i : i + CHUNK], mats[m, :, i : i + CHUNK],
                (((1,), (1,)), ((), ())), preferred_element_type=jnp.float32,
            )
        return total

    def middle(k):
        scale = inverse[:, :ranks] if ranks <= BLOCK else inverse[:, :1]
        pre = product(0) * scale
        dact = product(1)
        sig = jax.nn.sigmoid(pre)
        dpre = dact * sig * (1.0 + pre * (1.0 - sig))
        mid[0] = (dpre * scale).T.astype(jnp.bfloat16)
        mid[1] = (pre * sig).T.astype(jnp.bfloat16)

    def outer(k, m):
        rows = rows_h if m == 0 else rows_g

        def step(i, carry):
            into = pl.ds(pl.multiple_of(i * CHUNK, CHUNK), CHUNK)
            part = lax.dot_general(
                mid[m], rows[:, into], (((1,), (0,)), ((), ())), preferred_element_type=jnp.float32
            ).astype(jnp.bfloat16)
            for r in range(CHUNK // BLOCK):
                col = i * (CHUNK // BLOCK) + r
                for c in range(rows_k):
                    b = col * rows_k + c if m == 0 else blocks + c * rows_d + col
                    grads[k][b] = part[c * size : (c + 1) * size, r * BLOCK : (r + 1) * BLOCK]
            return carry

        lax.fori_loop(0, chunks, step, 0)

    def fill(k, part, z, p, terms, into=None):
        lay = red[k]
        n = lay.sizes[part] // 2
        first = lay.first(part)
        base = lay.start(part, z, p)

        def step(which, carry):
            dev = 2 * (4 * z + p) + which
            for i in range(n):
                entry = base + which * n + i
                value = grads[k][table_s[dev, first + i]]
                if terms:
                    value = value.astype(jnp.float32)
                    for term in terms:
                        value += term[k, entry].astype(jnp.float32)
                    value = value.astype(jnp.bfloat16)
                if into is None:
                    held[k, entry] = value
                else:
                    into[k, 2 * first + which * n + i] = value
            return carry

        lax.fori_loop(0, 2, step, 0)

    def give(k, part, z, p, buf, sem, peer, present=None):
        src = red[k].piece(held, k, part, z, p)
        send(src, red[k].piece(buf, k, part, z, p), sem, peer, present)

    def take(k, part, z, p, buf, sem):
        got(red[k].piece(buf, k, part, z, p), sem)

    def sem_second(k, part, z, passed):
        return second_sems.at[k, passed, z if part == 0 else depth]

    def sem_first(k, part, z):
        return first_sems.at[k, z if part == 0 else depth]

    def behind(d):
        if d > 0:
            return at.has_below, from_below, below_sems, at.above
        return at.has_above, from_above, above_sems, at.below

    def level_out(k, d):
        before, buf, sems, peer = behind(d)
        here = inside(d)

        def run():
            z = at.z + d

            def fills(terms):
                for p in range(4):
                    fill(k, 1, z, p, terms)

            def summed():
                got(red[k].level(buf, k, z), sems.at[k, 1, z])
                fills([buf])

            pl.when(jnp.logical_not(before))(lambda: fills([]))
            pl.when(before)(summed)
            send(
                red[k].level(held, k, z), red[k].level(buf, k, z), sems.at[k, 1, z],
                peer, lambda: here,
            )

        if red[k].sizes[1]:
            pl.when(here)(run)

    def beside(run):
        above, below = at.has_above, at.has_below
        pl.when(below & above)(lambda: run([from_below, from_above]))
        pl.when(below & jnp.logical_not(above))(lambda: run([from_below]))
        pl.when(above & jnp.logical_not(below))(lambda: run([from_above]))

    def second(k, d, which):
        z = (at.z + d) % depth
        p = at.diag if which else at.far
        fill(k, 0, z, p, [])
        give(k, 0, z, p, from_second, sem_second(k, 0, z, which), at.second)

    def first(k, d):
        z = (at.z + d) % depth
        take(k, 0, z, at.near, from_second, sem_second(k, 0, z, 1))
        fill(k, 0, z, at.near, [from_second])
        give(k, 0, z, at.near, from_first, sem_first(k, 0, z), at.first)

    def level_sums(k):
        if not red[k].sizes[1]:
            return
        for more, buf, sems in (
            (at.has_below, from_below, below_sems), (at.has_above, from_above, above_sems)
        ):
            pl.when(more)(
                lambda buf=buf, sems=sems: got(red[k].level(buf, k, at.z), sems.at[k, 1, at.z])
            )

        def run(terms):
            for p in (at.diag, at.far):
                fill(k, 1, at.z, p, terms)

        beside(run)
        for passed, p in ((1, at.diag), (0, at.far)):
            give(k, 1, at.z, p, from_second, sem_second(k, 1, at.z, passed), at.second)

    def level_first(k):
        if not red[k].sizes[1]:
            return
        take(k, 1, at.z, at.near, from_second, sem_second(k, 1, at.z, 1))
        beside(lambda terms: fill(k, 1, at.z, at.near, [from_second] + terms))
        give(k, 1, at.z, at.near, from_first, sem_first(k, 1, at.z), at.first)

    def line_out(k, d):
        before, buf, sems, peer = behind(d)
        here = inside(d)
        terms = [from_second, from_first]

        def run():
            z = at.z + d
            take(k, 0, z, at.own, from_second, sem_second(k, 0, z, 0))
            take(k, 0, z, at.own, from_first, sem_first(k, 0, z))

            def summed():
                take(k, 0, z, at.own, buf, sems.at[k, 0, z])
                fill(k, 0, z, at.own, terms + [buf])

            pl.when(jnp.logical_not(before))(lambda: fill(k, 0, z, at.own, terms))
            pl.when(before)(summed)
            give(k, 0, z, at.own, buf, sems.at[k, 0, z], peer, lambda: here)

        pl.when(here)(run)

    def finish(k):
        lay = red[k]
        for part in lay.parts[::-1]:
            take(k, part, at.z, at.own, from_second, sem_second(k, part, at.z, 0))
            take(k, part, at.z, at.own, from_first, sem_first(k, part, at.z))
        pl.when(at.has_below)(lambda: take(k, 0, at.z, at.own, from_below, below_sems.at[k, 0, at.z]))
        pl.when(at.has_above)(lambda: take(k, 0, at.z, at.own, from_above, above_sems.at[k, 0, at.z]))

        def run(terms):
            for part in lay.parts:
                fill(k, part, at.z, at.own, [from_second, from_first] + terms, final)

        beside(run)
        for part in lay.parts:
            n = lay.sizes[part] // 2
            piece = pl.ds(2 * lay.first(part) + (1 - core) * n, n)
            send(final.at[k, piece], twin.at[k, piece], twin_sems.at[k, part], at.sibling)

    def assemble(k):
        lay = red[k]
        for part in lay.parts:
            n = lay.sizes[part] // 2
            piece = pl.ds(2 * lay.first(part) + core * n, n)
            got(twin.at[k, piece], twin_sems.at[k, part])
        mine = pl.ds(pl.multiple_of(core * half + k * size, size), size)
        theirs = pl.ds(pl.multiple_of((1 - core) * half + k * size, size), size)
        for j in range(per):
            part = lay.part_of(j)
            entry = lay.first(part) + core * (lay.sizes[part] // 2) + 2 * j
            flat[j, mine, :] = final[k, entry]
            flat[j, theirs, :] = twin[k, entry]
            out[1, j, mine, :] = final[k, entry + 1]
            out[1, j, theirs, :] = twin[k, entry + 1]

    steps = {
        "gs": own_second, "gf": own_first, "gu": lambda k: own_line(k, 1),
        "gd": lambda k: own_line(k, -1), "gp": own_plane, "rows": load_rows,
        "near": near_own, "line": line, "nline": near_line, "pown": plane_own, "plane": plane,
        "side": side, "tables": tables, "scales": scales, "expand": expand, "middle": middle,
        "outer": outer, "lout": level_out, "second": second, "first": first,
        "lsum": level_sums, "lfirst": level_first, "zout": line_out, "finish": finish,
        "place": assemble,
    }
    for step in ORDER if depth == 4 else plain_order(depth):
        steps[step[0]](*step[1:])
    for j in range(per):
        out[0, j] = flat[j].T
    for n, (like, present) in enumerate(sends):

        def sent(n=n, like=like):
            remote(like(), like(), send_sems.at[n], load_sems.at[0], at.sibling).wait_send()

        if present is None:
            sent()
        else:
            pl.when(present())(sent)


def one_section(tokens, blocks_in, blocks_out, pos_in, pos_out, cotangent):
    devices = lax.axis_size("dp")
    per = blocks_in.shape[1]
    count, width = tokens.shape
    depth = devices // 8
    chips = devices // 2
    entries = 4 * per * chips
    sends = 8 * depth + SLICES * (15 + 14 * depth)
    size = BLOCK // 2 // SLICES
    ranks = RANK // BLOCK * size
    blocks = (width // BLOCK) * (RANK // BLOCK)
    dma = pltpu.SemaphoreType.DMA
    vmem = pltpu.VMEM
    anywhere = pl.BlockSpec(memory_space=pl.ANY)
    scalars = pl.BlockSpec(memory_space=pltpu.SMEM)
    local = pl.BlockSpec(memory_space=vmem)
    bf16, f32, i32 = jnp.bfloat16, jnp.float32, jnp.int32
    shards = (SLICES, entries, size, BLOCK)
    words = -(-(2 * blocks + 1) // BLOCK)
    words = -(-words // 8) * 8
    results = pl.pallas_call(
        functools.partial(fused_kernel, devices),
        out_shape=jax.ShapeDtypeStruct((2, per, BLOCK, BLOCK), bf16),
        in_specs=[scalars, scalars] + [anywhere] * 4,
        out_specs=local,
        scratch_shapes=[
            vmem((2, per, BLOCK, BLOCK), bf16),
            [vmem((entries + 1, size, BLOCK), bf16) for _ in range(SLICES)],
            vmem((SLICES, 2 * per, size, BLOCK), bf16),
            vmem((2 * count, width), bf16),
            vmem((2 * count, width), bf16),
            vmem((2, ranks, width), bf16),
            [vmem((2 * blocks + 1, size, BLOCK), bf16) for _ in range(SLICES)],
            vmem((2 * count, BLOCK), f32),
            vmem((devices, 8, BLOCK), i32),
            vmem((devices, BLOCK), i32),
            pltpu.SMEM((devices, BLOCK), i32),
            [vmem((words, BLOCK), i32) for _ in range(SLICES)],
            [pltpu.SMEM((words, BLOCK), i32) for _ in range(SLICES)],
            vmem((2, ranks, 2 * count), bf16),
            vmem(shards, bf16),
            vmem(shards, bf16),
            vmem(shards, bf16),
            vmem(shards, bf16),
            vmem(shards, bf16),
            vmem((SLICES, 4 * per, size, BLOCK), bf16),
            vmem((SLICES, 4 * per, size, BLOCK), bf16),
            vmem((per, BLOCK, BLOCK), bf16),
            dma((7 + SLICES,)),
            dma((sends,)),
            dma((SLICES, 2)),
            dma((SLICES, 2)),
            dma((chips + 1,)),
            dma((SLICES, chips + 4)),
            dma((SLICES, depth)),
            dma((SLICES, 2, depth + 1)),
            dma((SLICES, depth + 1)),
            dma((SLICES, 2, depth)),
            dma((SLICES, 2, depth)),
        ],
        compiler_params=pltpu.CompilerParams(
            collective_id=0, has_side_effects=True, vmem_limit_bytes=63 * 1024 * 1024
        ),
        name="fused_adapters",
    )(pos_in, pos_out, blocks_in[0], blocks_out[0], tokens, cotangent)
    return (results[0][None], results[1][None])


def solution(mesh):
    in_specs = (
        P("dp", None),
        P("section", "dp", None, None),
        P("section", "dp", None, None),
        P("section", "dp"),
        P("section", "dp"),
        P("dp", None),
    )
    out_specs = (P("section", "dp", None, None), P("section", "dp", None, None))
    body = one_section if mesh.shape["section"] == 1 else per_device
    return jax.shard_map(
        body, mesh=mesh, in_specs=in_specs, out_specs=out_specs, check_vma=False
    )
```

```python
import functools

import jax
import jax.numpy as jnp
from jax import lax
from jax.experimental import pallas as pl
from jax.experimental.pallas import tpu as pltpu
from jax.sharding import PartitionSpec as P

D = 8192
RANK = 512
BLOCK = 128
MICRO = 2


EPS = 1e-05


def from_behind(block, axis, distance):
    devices = range(lax.axis_size(axis))
    route = [(i - distance, i) for i in devices if i - distance in devices]
    return lax.ppermute(block, axis, route)


def expand(blocks, places, rows_b, cols_b):
    flat = jnp.zeros((rows_b * cols_b, BLOCK, BLOCK), blocks.dtype)
    flat = flat.at[places].set(blocks, mode="drop")
    return (
        flat.reshape(rows_b, cols_b, BLOCK, BLOCK)
        .transpose(0, 2, 1, 3)
        .reshape(rows_b * BLOCK, cols_b * BLOCK)
    )


def slot_grads(left, right, places, rows_b, cols_b):
    count = left.shape[0]
    valid = places < rows_b * cols_b
    row_block = jnp.where(valid, places // cols_b, 0).astype(jnp.int32)
    col_block = jnp.where(valid, places % cols_b, 0).astype(jnp.int32)
    left_blocks = jnp.take(left.reshape(count, rows_b, BLOCK), row_block, axis=1)
    right_blocks = jnp.take(right.reshape(count, cols_b, BLOCK), col_block, axis=1)
    result = jnp.einsum(
        "tjb,tjc->jbc", left_blocks, right_blocks, preferred_element_type=jnp.float32
    )
    return jnp.where(valid[:, None, None], result, 0.0)


def norm_parts(hidden):
    wide = hidden.astype(jnp.float32)
    scale = jnp.sqrt(jnp.mean(wide * wide, axis=-1, keepdims=True) + EPS)
    return (wide, scale)


def forward_layer(hidden, mat_a, mat_b):
    wide, scale = norm_parts(hidden)
    normed = (wide / scale).astype(jnp.bfloat16)
    pre = jnp.dot(normed, mat_a, preferred_element_type=jnp.float32)
    act = (pre * jax.nn.sigmoid(pre)).astype(jnp.bfloat16)
    return (wide + jnp.dot(act, mat_b, preferred_element_type=jnp.float32)).astype(jnp.bfloat16)


def backward_layer(hidden, upstream, mat_a, mat_b):
    wide, scale = norm_parts(hidden)
    unit = wide / scale
    normed = unit.astype(jnp.bfloat16)
    pre = jnp.dot(normed, mat_a, preferred_element_type=jnp.float32)
    sig = jax.nn.sigmoid(pre)
    act = (pre * sig).astype(jnp.bfloat16)
    dact = lax.dot_general(
        upstream, mat_b, (((1,), (1,)), ((), ())), preferred_element_type=jnp.float32
    )
    dpre = (dact * sig * (1.0 + pre * (1.0 - sig))).astype(jnp.bfloat16)
    dnorm = lax.dot_general(
        dpre, mat_a, (((1,), (1,)), ((), ())), preferred_element_type=jnp.float32
    )
    inner = jnp.mean(dnorm * unit, axis=-1, keepdims=True)
    earlier = (upstream.astype(jnp.float32) + (dnorm - unit * inner) / scale).astype(jnp.bfloat16)
    return (earlier, normed, dpre, act)


def store(stack, value, picked, active):
    updated = lax.dynamic_update_slice_in_dim(stack, value[None], picked, 0)
    return jnp.where(active, updated, stack)


def per_device(tokens, blocks_in, blocks_out, pos_in, pos_out, cotangent):
    sections = lax.axis_size("section")
    here = lax.axis_index("section")
    rows_d = D // BLOCK
    rows_k = RANK // BLOCK
    full_in, full_out, all_in, all_out = (
        lax.all_gather(blocks_in, "dp", axis=1, tiled=True),
        lax.all_gather(blocks_out, "dp", axis=1, tiled=True),
        lax.all_gather(pos_in, "dp", axis=1, tiled=True),
        lax.all_gather(pos_out, "dp", axis=1, tiled=True),
    )
    mat_a = expand(full_in[0], all_in[0], rows_d, rows_k)
    mat_b = expand(full_out[0], all_out[0], rows_k, rows_d)
    micro_rows = tokens.shape[0] // MICRO
    turns = MICRO + sections - 1
    saved = jnp.zeros((MICRO, micro_rows, D), jnp.bfloat16)
    carried = jnp.zeros((micro_rows, D), jnp.bfloat16)
    for turn in range(turns):
        micro = turn - here
        active = (micro >= 0) & (micro < MICRO)
        picked = jnp.clip(micro, 0, MICRO - 1)
        first = lax.dynamic_slice_in_dim(tokens, picked * micro_rows, micro_rows, 0)
        entering = jnp.where(here == 0, first, carried)
        saved = store(saved, entering, picked, active)
        if turn < turns - 1:
            leaving = lax.cond(
                active, lambda x: forward_layer(x, mat_a, mat_b), lambda x: x, entering
            )
            carried = from_behind(leaving, "section", 1)
    kept_normed = jnp.zeros((MICRO, micro_rows, D), jnp.bfloat16)
    kept_dpre = jnp.zeros((MICRO, micro_rows, RANK), jnp.bfloat16)
    kept_act = jnp.zeros((MICRO, micro_rows, RANK), jnp.bfloat16)
    kept_upper = jnp.zeros((MICRO, micro_rows, D), jnp.bfloat16)
    carried_grad = jnp.zeros((micro_rows, D), jnp.bfloat16)
    for turn in range(turns):
        micro = turn - (sections - 1 - here)
        active = (micro >= 0) & (micro < MICRO)
        picked = jnp.clip(micro, 0, MICRO - 1)
        last = lax.dynamic_slice_in_dim(cotangent, picked * micro_rows, micro_rows, 0)
        upstream = jnp.where(here == sections - 1, last, carried_grad)
        hidden = lax.dynamic_index_in_dim(saved, picked, 0, keepdims=False)

        def run_layer():
            return backward_layer(hidden, upstream, mat_a, mat_b)

        def skip_layer():
            return (
                upstream,
                jnp.zeros((micro_rows, D), jnp.bfloat16),
                jnp.zeros((micro_rows, RANK), jnp.bfloat16),
                jnp.zeros((micro_rows, RANK), jnp.bfloat16),
            )

        earlier, normed, dpre, act = lax.cond(active, run_layer, skip_layer)
        kept_normed = store(kept_normed, normed, picked, active)
        kept_dpre = store(kept_dpre, dpre, picked, active)
        kept_act = store(kept_act, act, picked, active)
        kept_upper = store(kept_upper, upstream, picked, active)
        if turn < turns - 1:
            carried_grad = from_behind(earlier, "section", -1)
    all_rows = MICRO * micro_rows
    terms_in = slot_grads(
        kept_normed.reshape(all_rows, D),
        kept_dpre.reshape(all_rows, RANK),
        all_in[0],
        rows_d,
        rows_k,
    )[None]
    terms_out = slot_grads(
        kept_act.reshape(all_rows, RANK),
        kept_upper.reshape(all_rows, D),
        all_out[0],
        rows_k,
        rows_d,
    )[None]
    sums_in, sums_out = (
        lax.psum_scatter(
            terms_in.astype(jnp.bfloat16), "dp", scatter_dimension=1, tiled=True
        ).astype(jnp.float32),
        lax.psum_scatter(
            terms_out.astype(jnp.bfloat16), "dp", scatter_dimension=1, tiled=True
        ).astype(jnp.float32),
    )
    return (sums_in.astype(jnp.bfloat16), sums_out.astype(jnp.bfloat16))


SLICES = 2
GATHER_PLANE = (1, 1)
REDUCE_PLANE = (1, 1)
CHUNK = 1024

def plain_order(depth):
    steps = []
    both = [d for r in range(1, depth) for d in (-r, r)]
    slices = range(SLICES)
    for k in slices:
        steps += [(name, k) for name in ("gs", "gf", "gu", "gd", "gp", "near")]
        steps += [("rows",)] if k == 0 else []
        steps += [("line", k, d) for d in both] + [("nline", k, d) for d in both]
        steps += [("pown", k)] + [("plane", k, d) for d in both] + [("side", k)]
        steps += [("tables",), ("scales",)] if k == 0 else []
        steps += [("expand", k, 0), ("expand", k, 1), ("middle", k), ("outer", k, 0), ("outer", k, 1)]
        steps += [("second", k, d, w) for d in range(depth) for w in (1, 0)]
    for k in slices:
        steps += [("lout", k, -d) for d in reversed(both)] + [("first", k, d) for d in range(depth)]
        steps += [("lsum", k), ("lfirst", k)] + [("zout", k, -d) for d in reversed(both)]
        steps += [("finish", k)]
    return steps + [("place", k) for k in slices]


ORDER = (
    ("gs", 0), ("gd", 0), ("gs", 1), ("gf", 0), ("gp", 0), ("rows",), ("gu", 0), ("near", 0),
    ("line", 0, 1), ("line", 0, -1), ("gf", 1), ("gu", 1), ("line", 0, -2), ("line", 0, 2),
    ("pown", 0), ("scales",), ("nline", 0, -1), ("line", 0, -3), ("nline", 0, 1),
    ("plane", 0, -1), ("line", 0, 3), ("plane", 0, 1), ("nline", 0, -2), ("nline", 0, 3),
    ("gd", 1), ("nline", 0, -3), ("plane", 0, -2), ("nline", 0, 2), ("plane", 0, 2), ("gp", 1),
    ("near", 1), ("line", 1, 1), ("plane", 0, -3), ("line", 1, -1), ("plane", 0, 3),
    ("side", 0), ("tables",), ("line", 1, 2), ("line", 1, -2), ("expand", 0, 0),
    ("nline", 1, 1), ("pown", 1), ("expand", 0, 1), ("nline", 1, -1), ("line", 1, 3),
    ("middle", 0), ("nline", 1, -2), ("plane", 1, 1), ("nline", 1, 2), ("line", 1, -3),
    ("plane", 1, -1), ("outer", 0, 0), ("nline", 1, -3), ("nline", 1, 3), ("outer", 0, 1),
    ("plane", 1, -2), ("plane", 1, 2), ("second", 0, 3, 1), ("lout", 0, -3), ("lout", 0, 3),
    ("second", 0, 1, 1), ("second", 0, 2, 1), ("side", 1), ("second", 0, 3, 0),
    ("second", 0, 1, 0), ("second", 0, 2, 0), ("plane", 1, 3), ("plane", 1, -3),
    ("expand", 1, 0), ("first", 0, 3), ("lout", 0, -2), ("lout", 0, 2), ("expand", 1, 1),
    ("first", 0, 1), ("middle", 1), ("lout", 0, -1), ("lout", 0, 1), ("first", 0, 2),
    ("outer", 1, 0), ("zout", 0, 3), ("outer", 1, 1), ("lout", 1, -3), ("second", 1, 3, 1),
    ("second", 1, 1, 1), ("second", 1, 2, 1), ("lout", 1, 3), ("second", 1, 1, 0),
    ("second", 1, 3, 0), ("zout", 0, -3), ("second", 1, 2, 0), ("lout", 1, -2), ("first", 1, 3),
    ("lout", 1, 2), ("first", 1, 1), ("second", 1, 0, 1), ("lout", 1, -1), ("zout", 1, -3),
    ("lout", 1, 1), ("zout", 0, 2), ("lsum", 0), ("zout", 1, 3), ("first", 1, 2),
    ("second", 0, 0, 1), ("zout", 0, -2), ("zout", 1, -2), ("zout", 0, 1), ("first", 1, 0),
    ("second", 0, 0, 0), ("lsum", 1), ("zout", 0, -1), ("zout", 1, 2), ("first", 0, 0),
    ("second", 1, 0, 0), ("zout", 1, -1), ("zout", 1, 1), ("lfirst", 0), ("lfirst", 1),
    ("finish", 0), ("finish", 1), ("place", 0), ("place", 1),
)


class Place:
    def __init__(self, devices):
        me = lax.axis_index("dp")
        self.depth = devices // 8
        self.me = me
        self.core = me % 2
        self.chip = me // 2
        x = self.chip % 2
        y = (self.chip // 2) % 2
        self.z = self.chip // 4
        dx = 1 - 2 * x
        dy = 2 * (1 - 2 * y)
        first = (1 - self.core) * dx + self.core * dy
        second = (1 - self.core) * dy + self.core * dx
        self.own = self.chip % 4
        self.near = self.own + first
        self.far = self.own + second
        self.diag = self.own + first + second
        self.sibling = me + 1 - 2 * self.core
        self.first = me + 2 * first
        self.second = me + 2 * second
        self.above = me + 8
        self.below = me - 8
        self.has_above = self.z + 1 < self.depth
        self.has_below = self.z >= 1

    def knock(self):
        barrier = pltpu.get_barrier_semaphore()

        def signal(peer):
            pl.semaphore_signal(
                barrier, inc=1, device_id={"dp": peer}, device_id_type=pl.DeviceIdType.MESH
            )

        for peer in (self.sibling, self.first, self.second):
            signal(peer)
        pl.when(self.has_above)(lambda: signal(self.above))
        pl.when(self.has_below)(lambda: signal(self.below))

        peers = 3 + self.has_above.astype(jnp.int32) + self.has_below.astype(jnp.int32)
        return lambda: pl.semaphore_wait(barrier, peers)


def remote(src, dst, send, recv, peer):
    return pltpu.make_async_remote_copy(
        src_ref=src,
        dst_ref=dst,
        send_sem=send,
        recv_sem=recv,
        device_id={"dp": peer},
        device_id_type=pl.DeviceIdType.MESH,
    )


class Layout:
    def __init__(self, devices, per, odd):
        self.split = per - odd
        self.depth = devices // 8
        self.sizes = (4 * (per - odd), 4 * odd)
        self.parts = (0, 1) if odd else (0,)
        self.plane = 16 * per
        self.total = self.depth * self.plane

    def part_of(self, j):
        return 0 if j < self.split else 1

    def first(self, part):
        return 0 if part == 0 else 2 * self.split

    def start(self, part, z, p):
        line, odd = self.sizes
        return z * self.plane + (p * line if part == 0 else 4 * line + p * odd)

    def piece(self, buf, k, part, z, p):
        span = pl.ds(self.start(part, z, p), self.sizes[part])
        return buf.at[span] if k is None else buf.at[k, span]

    def level(self, buf, k, z):
        line, odd = self.sizes
        span = pl.ds(z * self.plane + 4 * line, 4 * odd)
        return buf.at[span] if k is None else buf.at[k, span]


def fused_kernel(devices, pos_in, pos_out, blocks_in, blocks_out, tokens, cotangent, out,
                 own, full, stage, rows_h, rows_g, mats, grads, inverse,
                 tags, table, table_s, begin, begin_s, mid,
                 held, from_second, from_first, from_below, from_above, final, twin, flat,
                 load_sems, send_sems, group_sems, pair_sems, twin_sems, tag_sems, gather_sems, level_sems,
                 second_sems, first_sems, below_sems, above_sems):
    at = Place(devices)
    depth = at.depth
    core = at.core
    per = blocks_in.shape[0]
    gat = [Layout(devices, per, odd) for odd in GATHER_PLANE]
    red = [Layout(devices, per, odd) for odd in REDUCE_PLANE]
    count, width = tokens.shape
    size = full[0].shape[1]
    half = BLOCK // 2
    rows_k = RANK // BLOCK
    rows_d = width // BLOCK
    blocks = rows_k * rows_d
    ranks = rows_k * size
    chunks = width // CHUNK
    sends = []
    waits = []
    groups = {}
    singles = []

    def groups_at(name):
        return group_sems.at[groups[name]]


    def like(kind, rows):
        if kind == "tag":
            return tags.at[0]
        return tags.at[pl.ds(0, rows)] if kind == "tags" else full[0].at[pl.ds(0, rows)]

    def send(src, dst, recv, peer, present=None, group=None):
        whole = src.dtype == jnp.int32
        kind = ("tag" if len(src.shape) == 2 else "tags") if whole else "blocks"
        if group is not None:
            name, copies = group
            name += (kind,)
            if name not in groups:
                groups[name] = len(groups)
                sends.append((True, groups[name], kind, copies * src.shape[0], None))
            sem = groups_at(name)
        else:
            singles.append(present)
            sem = send_sems.at[len(singles) - 1]
            sends.append((False, len(singles) - 1, kind, src.shape[0], present))
        remote(src, dst, sem, recv, peer).start()

    def got(buf, sem):
        remote(buf, buf, send_sems.at[0], sem, at.sibling).wait_recv()

    wait_peers = at.knock()
    own_loads = [
        pltpu.make_async_copy(blocks_in, own.at[0], load_sems.at[5]),
        pltpu.make_async_copy(blocks_out, own.at[1], load_sems.at[6]),
    ]
    for copy in own_loads:
        copy.start()

    own_rows = pl.ds(pl.multiple_of(core * count, count), count)
    local = [
        pltpu.make_async_copy(tokens, rows_h.at[own_rows], load_sems.at[0]),
        pltpu.make_async_copy(cotangent, rows_g.at[own_rows], load_sems.at[1]),
    ]
    for copy in local:
        copy.start()

    lanes = lax.broadcasted_iota(jnp.int32, tags.shape[1:], 1)
    row = jnp.full(tags.shape[1:], 2 * blocks, jnp.int32)
    for j in range(per):
        place = pos_in[0, j]
        row = jnp.where(lanes == 2 * j, jnp.where(place < blocks, place, 2 * blocks), row)
        row = jnp.where(lanes == 2 * j + 1, pos_out[0, j] + blocks, row)
    tags[at.me] = row

    for copy in own_loads:
        copy.wait()
    for j in range(per):
        flat[0] = own[0, j].T
        flat[1] = own[1, j]
        for k in range(SLICES):
            lay = gat[k]
            part = lay.part_of(j)
            base = lay.start(part, at.z, at.own) + core * (lay.sizes[part] // 2)
            base += 2 * j - lay.first(part)
            keep = pl.ds(pl.multiple_of(core * half + k * size, size), size)
            give = pl.ds(pl.multiple_of((1 - core) * half + k * size, size), size)
            for m in range(2):
                full[k][base + m] = flat[m, keep, :]
                stage[k, 2 * j + m] = flat[m, give, :]
    for k in range(SLICES):
        full[k][gat[k].total] = jnp.zeros((size, BLOCK), jnp.bfloat16)
        grads[k][2 * blocks] = jnp.zeros((size, BLOCK), jnp.bfloat16)

    wait_peers()

    def pair(k, start):
        lay = gat[k]
        for part in lay.parts:
            n = lay.sizes[part] // 2
            base = lay.start(part, at.z, at.own) + core * n
            src, dst = stage.at[k, pl.ds(lay.first(part), n)], full[k].at[pl.ds(base, n)]
            if start:
                send(src, dst, pair_sems.at[k, part], at.sibling)
            else:
                got(src, pair_sems.at[k, part])

    send(tags.at[at.me], tags.at[at.me], tag_sems.at[4 * depth], at.sibling)
    for k in range(SLICES):
        pair(k, True)

    def tag_piece(z, p):
        return tags.at[pl.ds(2 * (4 * z + p), 2)]

    def push(k, part, z, p, peer, present=None):
        group = None
        if peer is at.second:
            group = (("gather", k, part, 2), 2 * depth if part == 0 else 2)
        elif peer is at.first:
            group = (("gather", k, part, 1), depth if part == 0 else 1)
        if k == 0 and part == 0:
            piece = tag_piece(z, p)
            send(piece, piece, tag_sems.at[4 * z + p], peer, present, group)
        piece = gat[k].piece(full[k], None, part, z, p)
        send(piece, piece, gather_sems.at[k, 4 * z + p if part == 0 else 4 * depth + p], peer, present, group)

    def arrived(k, part, z, p):
        if k == 0 and part == 0:
            got(tag_piece(z, p), tag_sems.at[4 * z + p])
        got(gat[k].piece(full[k], None, part, z, p), gather_sems.at[k, 4 * z + p if part == 0 else 4 * depth + p])

    def inside(d):
        return (at.z + d < depth) if d > 0 else (at.z + d >= 0)

    def onward(d):
        return (at.has_below, at.below) if d > 0 else (at.has_above, at.above)

    def away(d):
        return (at.has_above, at.above) if d > 0 else (at.has_below, at.below)

    def own_second(k):
        pair(k, False)
        if k == 0:
            got(tags.at[at.me], tag_sems.at[4 * depth])
        push(k, 0, at.z, at.own, at.second)

    def own_first(k):
        push(k, 0, at.z, at.own, at.first)

    def own_line(k, d):
        more, peer = away(d)
        pl.when(more)(lambda: push(k, 0, at.z, at.own, peer, lambda: more))

    def own_plane(k):
        for part in gat[k].parts[1:]:
            push(k, part, at.z, at.own, at.second)
            push(k, part, at.z, at.own, at.first)

    def near_own(k):
        for part in gat[k].parts:
            arrived(k, part, at.z, at.near)
            push(k, part, at.z, at.near, at.second)

    def line(k, d):
        more, peer = onward(d)
        here = inside(d)

        def run():
            z = at.z + d
            arrived(k, 0, z, at.own)
            pl.when(more)(lambda: push(k, 0, z, at.own, peer, lambda: more & here))
            push(k, 0, z, at.own, at.second, lambda: here)
            push(k, 0, z, at.own, at.first, lambda: here)

        pl.when(here)(run)

    def near_line(k, d):
        here = inside(d)

        def run():
            arrived(k, 0, at.z + d, at.near)
            push(k, 0, at.z + d, at.near, at.second, lambda: here)

        pl.when(here)(run)

    def push_level(k, z, peer, present):
        piece = gat[k].level(full[k], None, z)
        send(piece, piece, level_sems.at[k, z], peer, present)

    def plane_own(k):
        for part in gat[k].parts:
            for p in (at.far, at.diag):
                arrived(k, part, at.z, p)
        if gat[k].sizes[1]:
            for more, peer in (away(1), away(-1)):
                pl.when(more)(lambda more=more, peer=peer: push_level(k, at.z, peer, lambda: more))

    def plane(k, d):
        more, peer = onward(d)
        here = inside(d)

        def run():
            got(gat[k].level(full[k], None, at.z + d), level_sems.at[k, at.z + d])
            pl.when(more)(lambda: push_level(k, at.z + d, peer, lambda: more & here))

        if gat[k].sizes[1]:
            pl.when(here)(run)

    def side(k):
        for d in range(1 - depth, depth):

            def run(d=d):
                for p in (at.far, at.diag):
                    arrived(k, 0, at.z + d, p)

            if d:
                pl.when(inside(d))(run)

    def load_rows():
        swap = [
            remote(tokens, rows_h.at[own_rows], load_sems.at[7 + SLICES], load_sems.at[2], at.sibling),
            remote(cotangent, rows_g.at[own_rows], load_sems.at[8 + SLICES], load_sems.at[3], at.sibling),
        ]
        for copy in swap:
            copy.start()
        waits.extend(swap)

    def scales():
        for copy in local:
            copy.wait()
        for copy in waits:
            copy.wait_recv()
        total = jnp.zeros((2 * count, BLOCK), jnp.float32)
        for i in range(0, width, BLOCK):
            wide = rows_h[:, i : i + BLOCK].astype(jnp.float32)
            total += wide * wide
        scale = jnp.sqrt(jnp.sum(total, axis=-1, keepdims=True) / width + EPS)
        inverse[...] = jnp.broadcast_to(1.0 / scale, inverse.shape)

    def tables():
        table[...] = tags[:, 0, :]
        copy = pltpu.make_async_copy(table, table_s, load_sems.at[4])
        copy.start()
        copy.wait()
        shape = begin[0].shape
        numbers = lax.broadcasted_iota(jnp.int32, shape, 0) * BLOCK
        numbers += lax.broadcasted_iota(jnp.int32, shape, 1)

        kinds = {lay.split: lay for lay in gat}

        def scan(dev, found):
            z, p, which = dev // 8, (dev // 2) % 4, dev % 2
            bases = [
                [lay.start(part, z, p) + which * (lay.sizes[part] // 2) for part in range(2)]
                for lay in kinds.values()
            ]
            found = list(found)
            for lane in range(2 * per):
                same = numbers == table_s[dev, lane]
                for n, lay in enumerate(kinds.values()):
                    part = lay.part_of(lane // 2)
                    entry = bases[n][part] + (lane - lay.first(part))
                    found[n] = jnp.where(same, entry, found[n])
            return tuple(found)

        found = lax.fori_loop(
            0, devices, scan,
            tuple(jnp.full(shape, lay.total, jnp.int32) for lay in kinds.values()),
        )
        found = dict(zip(kinds, found))
        copies = []
        for k in range(SLICES):
            begin[k][...] = found[gat[k].split]
            copies.append(pltpu.make_async_copy(begin[k], begin_s[k], load_sems.at[7 + k]))
            copies[k].start()
        for copy in copies:
            copy.wait()

    def expand(k, m):
        group = BLOCK // rows_k

        def step(low, carry, high):
            r = high * group + low
            into = pl.ds(pl.multiple_of(r * BLOCK, BLOCK), BLOCK)
            found = []
            for c in range(rows_k):
                if m == 0:
                    at_c = begin_s[k][high, low * rows_k + c]
                else:
                    b = blocks + c * rows_d + high * group
                    at_c = begin_s[k][b // BLOCK, b % BLOCK + low]
                found.append(full[k][at_c])
            for c in range(rows_k):
                mats[m, c * size : (c + 1) * size, into] = found[c]
            return carry

        for high in range(rows_d // group):
            lax.fori_loop(0, group, functools.partial(step, high=high), 0, unroll=4)

    def product(m):
        rows = rows_h if m == 0 else rows_g
        total = jnp.zeros((2 * count, ranks), jnp.float32)
        for i in range(0, width, CHUNK):
            total += lax.dot_general(
                rows[:, i : i + CHUNK], mats[m, :, i : i + CHUNK],
                (((1,), (1,)), ((), ())), preferred_element_type=jnp.float32,
            )
        return total

    def middle(k):
        scale = inverse[:, :ranks] if ranks <= BLOCK else inverse[:, :1]
        pre = product(0) * scale
        dact = product(1)
        sig = jax.nn.sigmoid(pre)
        dpre = dact * sig * (1.0 + pre * (1.0 - sig))
        mid[0] = (dpre * scale).T.astype(jnp.bfloat16)
        mid[1] = (pre * sig).T.astype(jnp.bfloat16)

    def outer(k, m):
        rows = rows_h if m == 0 else rows_g

        def step(i, carry):
            into = pl.ds(pl.multiple_of(i * CHUNK, CHUNK), CHUNK)
            part = lax.dot_general(
                mid[m], rows[:, into], (((1,), (0,)), ((), ())), preferred_element_type=jnp.float32
            ).astype(jnp.bfloat16)
            for r in range(CHUNK // BLOCK):
                col = i * (CHUNK // BLOCK) + r
                for c in range(rows_k):
                    b = col * rows_k + c if m == 0 else blocks + c * rows_d + col
                    grads[k][b] = part[c * size : (c + 1) * size, r * BLOCK : (r + 1) * BLOCK]
            return carry

        lax.fori_loop(0, chunks, step, 0)

    def fill(k, part, z, p, terms, into=None):
        lay = red[k]
        n = lay.sizes[part] // 2
        first = lay.first(part)
        base = lay.start(part, z, p)

        def step(which, carry):
            dev = 2 * (4 * z + p) + which
            for i in range(n):
                entry = base + which * n + i
                value = grads[k][table_s[dev, first + i]]
                if terms:
                    value = value.astype(jnp.float32)
                    for term in terms:
                        value += term[k, entry].astype(jnp.float32)
                    value = value.astype(jnp.bfloat16)
                if into is None:
                    held[k, entry] = value
                else:
                    into[k, 2 * first + which * n + i] = value
            return carry

        lax.fori_loop(0, 2, step, 0)

    def give(k, part, z, p, buf, sem, peer, present=None):
        src = red[k].piece(held, k, part, z, p)
        group = None
        if peer is at.second:
            group = (("sums", k, part, 2), 2 * depth if part == 0 else 2)
        elif peer is at.first:
            group = (("sums", k, part, 1), depth if part == 0 else 1)
        send(src, red[k].piece(buf, k, part, z, p), sem, peer, present, group)

    def take(k, part, z, p, buf, sem):
        got(red[k].piece(buf, k, part, z, p), sem)

    def sem_second(k, part, z, passed):
        return second_sems.at[k, passed, z if part == 0 else depth]

    def sem_first(k, part, z):
        return first_sems.at[k, z if part == 0 else depth]

    def behind(d):
        if d > 0:
            return at.has_below, from_below, below_sems, at.above
        return at.has_above, from_above, above_sems, at.below

    def level_out(k, d):
        before, buf, sems, peer = behind(d)
        here = inside(d)

        def run():
            z = at.z + d

            def fills(terms):
                for p in range(4):
                    fill(k, 1, z, p, terms)

            def summed():
                got(red[k].level(buf, k, z), sems.at[k, 1, z])
                fills([buf])

            pl.when(jnp.logical_not(before))(lambda: fills([]))
            pl.when(before)(summed)
            send(
                red[k].level(held, k, z), red[k].level(buf, k, z), sems.at[k, 1, z],
                peer, lambda: here,
            )

        if red[k].sizes[1]:
            pl.when(here)(run)

    def beside(run):
        above, below = at.has_above, at.has_below
        pl.when(below & above)(lambda: run([from_below, from_above]))
        pl.when(below & jnp.logical_not(above))(lambda: run([from_below]))
        pl.when(above & jnp.logical_not(below))(lambda: run([from_above]))

    def second(k, d, which):
        z = (at.z + d) % depth
        p = at.diag if which else at.far
        fill(k, 0, z, p, [])
        give(k, 0, z, p, from_second, sem_second(k, 0, z, which), at.second)

    def first(k, d):
        z = (at.z + d) % depth
        take(k, 0, z, at.near, from_second, sem_second(k, 0, z, 1))
        fill(k, 0, z, at.near, [from_second])
        give(k, 0, z, at.near, from_first, sem_first(k, 0, z), at.first)

    def level_sums(k):
        if not red[k].sizes[1]:
            return
        for more, buf, sems in (
            (at.has_below, from_below, below_sems), (at.has_above, from_above, above_sems)
        ):
            pl.when(more)(
                lambda buf=buf, sems=sems: got(red[k].level(buf, k, at.z), sems.at[k, 1, at.z])
            )

        def run(terms):
            for p in (at.diag, at.far):
                fill(k, 1, at.z, p, terms)

        beside(run)
        for passed, p in ((1, at.diag), (0, at.far)):
            give(k, 1, at.z, p, from_second, sem_second(k, 1, at.z, passed), at.second)

    def level_first(k):
        if not red[k].sizes[1]:
            return
        take(k, 1, at.z, at.near, from_second, sem_second(k, 1, at.z, 1))
        beside(lambda terms: fill(k, 1, at.z, at.near, [from_second] + terms))
        give(k, 1, at.z, at.near, from_first, sem_first(k, 1, at.z), at.first)

    def line_out(k, d):
        before, buf, sems, peer = behind(d)
        here = inside(d)
        terms = [from_second, from_first]

        def run():
            z = at.z + d
            take(k, 0, z, at.own, from_second, sem_second(k, 0, z, 0))
            take(k, 0, z, at.own, from_first, sem_first(k, 0, z))

            def summed():
                take(k, 0, z, at.own, buf, sems.at[k, 0, z])
                fill(k, 0, z, at.own, terms + [buf])

            pl.when(jnp.logical_not(before))(lambda: fill(k, 0, z, at.own, terms))
            pl.when(before)(summed)
            give(k, 0, z, at.own, buf, sems.at[k, 0, z], peer, lambda: here)

        pl.when(here)(run)

    def finish(k):
        lay = red[k]
        for part in lay.parts[::-1]:
            take(k, part, at.z, at.own, from_second, sem_second(k, part, at.z, 0))
            take(k, part, at.z, at.own, from_first, sem_first(k, part, at.z))
        pl.when(at.has_below)(lambda: take(k, 0, at.z, at.own, from_below, below_sems.at[k, 0, at.z]))
        pl.when(at.has_above)(lambda: take(k, 0, at.z, at.own, from_above, above_sems.at[k, 0, at.z]))

        def run(terms):
            for part in lay.parts:
                fill(k, part, at.z, at.own, [from_second, from_first] + terms, final)

        beside(run)
        for part in lay.parts:
            n = lay.sizes[part] // 2
            piece = pl.ds(2 * lay.first(part) + (1 - core) * n, n)
            send(final.at[k, piece], twin.at[k, piece], twin_sems.at[k, part], at.sibling)

    def assemble(k):
        lay = red[k]
        for part in lay.parts:
            n = lay.sizes[part] // 2
            piece = pl.ds(2 * lay.first(part) + core * n, n)
            got(twin.at[k, piece], twin_sems.at[k, part])
        mine = pl.ds(pl.multiple_of(core * half + k * size, size), size)
        theirs = pl.ds(pl.multiple_of((1 - core) * half + k * size, size), size)
        for j in range(per):
            part = lay.part_of(j)
            entry = lay.first(part) + core * (lay.sizes[part] // 2) + 2 * j
            flat[j, mine, :] = final[k, entry]
            flat[j, theirs, :] = twin[k, entry]
            out[1, j, mine, :] = final[k, entry + 1]
            out[1, j, theirs, :] = twin[k, entry + 1]

    steps = {
        "gs": own_second, "gf": own_first, "gu": lambda k: own_line(k, 1),
        "gd": lambda k: own_line(k, -1), "gp": own_plane, "rows": load_rows,
        "near": near_own, "line": line, "nline": near_line, "pown": plane_own, "plane": plane,
        "side": side, "tables": tables, "scales": scales, "expand": expand, "middle": middle,
        "outer": outer, "lout": level_out, "second": second, "first": first,
        "lsum": level_sums, "lfirst": level_first, "zout": line_out, "finish": finish,
        "place": assemble,
    }
    for step in ORDER if depth == 4 else plain_order(depth):
        steps[step[0]](*step[1:])
    for j in range(per):
        out[0, j] = flat[j].T
    for shared, n, kind, rows, present in sends:

        def sent(shared=shared, n=n, kind=kind, rows=rows):
            piece = like(kind, rows)
            sem = group_sems.at[n] if shared else send_sems.at[n]
            remote(piece, piece, sem, load_sems.at[0], at.sibling).wait_send()

        if present is None:
            sent()
        else:
            pl.when(present())(sent)
    for copy in waits:
        copy.wait_send()


def one_section(tokens, blocks_in, blocks_out, pos_in, pos_out, cotangent):
    devices = lax.axis_size("dp")
    per = blocks_in.shape[1]
    count, width = tokens.shape
    depth = devices // 8
    chips = devices // 2
    entries = 4 * per * chips
    sends = 1 + 2 * depth + SLICES * 8 * depth
    shared = 8 * SLICES + 2
    size = BLOCK // 2 // SLICES
    ranks = RANK // BLOCK * size
    blocks = (width // BLOCK) * (RANK // BLOCK)
    dma = pltpu.SemaphoreType.DMA
    vmem = pltpu.VMEM
    anywhere = pl.BlockSpec(memory_space=pl.ANY)
    scalars = pl.BlockSpec(memory_space=pltpu.SMEM)
    local = pl.BlockSpec(memory_space=vmem)
    bf16, f32, i32 = jnp.bfloat16, jnp.float32, jnp.int32
    shards = (SLICES, entries, size, BLOCK)
    words = -(-(2 * blocks + 1) // BLOCK)
    words = -(-words // 8) * 8
    results = pl.pallas_call(
        functools.partial(fused_kernel, devices),
        out_shape=jax.ShapeDtypeStruct((2, per, BLOCK, BLOCK), bf16),
        in_specs=[scalars, scalars] + [anywhere] * 4,
        out_specs=local,
        scratch_shapes=[
            vmem((2, per, BLOCK, BLOCK), bf16),
            [vmem((entries + 1, size, BLOCK), bf16) for _ in range(SLICES)],
            vmem((SLICES, 2 * per, size, BLOCK), bf16),
            vmem((2 * count, width), bf16),
            vmem((2 * count, width), bf16),
            vmem((2, ranks, width), bf16),
            [vmem((2 * blocks + 1, size, BLOCK), bf16) for _ in range(SLICES)],
            vmem((2 * count, BLOCK), f32),
            vmem((devices, 8, BLOCK), i32),
            vmem((devices, BLOCK), i32),
            pltpu.SMEM((devices, BLOCK), i32),
            [vmem((words, BLOCK), i32) for _ in range(SLICES)],
            [pltpu.SMEM((words, BLOCK), i32) for _ in range(SLICES)],
            vmem((2, ranks, 2 * count), bf16),
            vmem(shards, bf16),
            vmem(shards, bf16),
            vmem(shards, bf16),
            vmem(shards, bf16),
            vmem(shards, bf16),
            vmem((SLICES, 4 * per, size, BLOCK), bf16),
            vmem((SLICES, 4 * per, size, BLOCK), bf16),
            vmem((per, BLOCK, BLOCK), bf16),
            dma((9 + SLICES,)),
            dma((sends,)),
            dma((shared,)),
            dma((SLICES, 2)),
            dma((SLICES, 2)),
            dma((chips + 1,)),
            dma((SLICES, chips + 4)),
            dma((SLICES, depth)),
            dma((SLICES, 2, depth + 1)),
            dma((SLICES, depth + 1)),
            dma((SLICES, 2, depth)),
            dma((SLICES, 2, depth)),
        ],
        compiler_params=pltpu.CompilerParams(
            collective_id=0, has_side_effects=True, vmem_limit_bytes=63 * 1024 * 1024
        ),
        name="fused_adapters",
    )(pos_in, pos_out, blocks_in[0], blocks_out[0], tokens, cotangent)
    return (results[0][None], results[1][None])


def solution(mesh):
    in_specs = (
        P("dp", None),
        P("section", "dp", None, None),
        P("section", "dp", None, None),
        P("section", "dp"),
        P("section", "dp"),
        P("dp", None),
    )
    out_specs = (P("section", "dp", None, None), P("section", "dp", None, None))
    body = one_section if mesh.shape["section"] == 1 else per_device
    return jax.shard_map(
        body, mesh=mesh, in_specs=in_specs, out_specs=out_specs, check_vma=False
    )
```

```python
import functools

import jax
import jax.numpy as jnp
from jax import lax
from jax.experimental import pallas as pl
from jax.experimental.pallas import tpu as pltpu
from jax.sharding import PartitionSpec as P

D = 8192
RANK = 512
BLOCK = 128
MICRO = 2


EPS = 1e-05


def from_behind(block, axis, distance):
    devices = range(lax.axis_size(axis))
    route = [(i - distance, i) for i in devices if i - distance in devices]
    return lax.ppermute(block, axis, route)


def expand(blocks, places, rows_b, cols_b):
    flat = jnp.zeros((rows_b * cols_b, BLOCK, BLOCK), blocks.dtype)
    flat = flat.at[places].set(blocks, mode="drop")
    return (
        flat.reshape(rows_b, cols_b, BLOCK, BLOCK)
        .transpose(0, 2, 1, 3)
        .reshape(rows_b * BLOCK, cols_b * BLOCK)
    )


def slot_grads(left, right, places, rows_b, cols_b):
    count = left.shape[0]
    valid = places < rows_b * cols_b
    row_block = jnp.where(valid, places // cols_b, 0).astype(jnp.int32)
    col_block = jnp.where(valid, places % cols_b, 0).astype(jnp.int32)
    left_blocks = jnp.take(left.reshape(count, rows_b, BLOCK), row_block, axis=1)
    right_blocks = jnp.take(right.reshape(count, cols_b, BLOCK), col_block, axis=1)
    result = jnp.einsum(
        "tjb,tjc->jbc", left_blocks, right_blocks, preferred_element_type=jnp.float32
    )
    return jnp.where(valid[:, None, None], result, 0.0)


def norm_parts(hidden):
    wide = hidden.astype(jnp.float32)
    scale = jnp.sqrt(jnp.mean(wide * wide, axis=-1, keepdims=True) + EPS)
    return (wide, scale)


def forward_layer(hidden, mat_a, mat_b):
    wide, scale = norm_parts(hidden)
    normed = (wide / scale).astype(jnp.bfloat16)
    pre = jnp.dot(normed, mat_a, preferred_element_type=jnp.float32)
    act = (pre * jax.nn.sigmoid(pre)).astype(jnp.bfloat16)
    return (wide + jnp.dot(act, mat_b, preferred_element_type=jnp.float32)).astype(jnp.bfloat16)


def backward_layer(hidden, upstream, mat_a, mat_b):
    wide, scale = norm_parts(hidden)
    unit = wide / scale
    normed = unit.astype(jnp.bfloat16)
    pre = jnp.dot(normed, mat_a, preferred_element_type=jnp.float32)
    sig = jax.nn.sigmoid(pre)
    act = (pre * sig).astype(jnp.bfloat16)
    dact = lax.dot_general(
        upstream, mat_b, (((1,), (1,)), ((), ())), preferred_element_type=jnp.float32
    )
    dpre = (dact * sig * (1.0 + pre * (1.0 - sig))).astype(jnp.bfloat16)
    dnorm = lax.dot_general(
        dpre, mat_a, (((1,), (1,)), ((), ())), preferred_element_type=jnp.float32
    )
    inner = jnp.mean(dnorm * unit, axis=-1, keepdims=True)
    earlier = (upstream.astype(jnp.float32) + (dnorm - unit * inner) / scale).astype(jnp.bfloat16)
    return (earlier, normed, dpre, act)


def store(stack, value, picked, active):
    updated = lax.dynamic_update_slice_in_dim(stack, value[None], picked, 0)
    return jnp.where(active, updated, stack)


def per_device(tokens, blocks_in, blocks_out, pos_in, pos_out, cotangent):
    sections = lax.axis_size("section")
    here = lax.axis_index("section")
    rows_d = D // BLOCK
    rows_k = RANK // BLOCK
    full_in, full_out, all_in, all_out = (
        lax.all_gather(blocks_in, "dp", axis=1, tiled=True),
        lax.all_gather(blocks_out, "dp", axis=1, tiled=True),
        lax.all_gather(pos_in, "dp", axis=1, tiled=True),
        lax.all_gather(pos_out, "dp", axis=1, tiled=True),
    )
    mat_a = expand(full_in[0], all_in[0], rows_d, rows_k)
    mat_b = expand(full_out[0], all_out[0], rows_k, rows_d)
    micro_rows = tokens.shape[0] // MICRO
    turns = MICRO + sections - 1
    saved = jnp.zeros((MICRO, micro_rows, D), jnp.bfloat16)
    carried = jnp.zeros((micro_rows, D), jnp.bfloat16)
    for turn in range(turns):
        micro = turn - here
        active = (micro >= 0) & (micro < MICRO)
        picked = jnp.clip(micro, 0, MICRO - 1)
        first = lax.dynamic_slice_in_dim(tokens, picked * micro_rows, micro_rows, 0)
        entering = jnp.where(here == 0, first, carried)
        saved = store(saved, entering, picked, active)
        if turn < turns - 1:
            leaving = lax.cond(
                active, lambda x: forward_layer(x, mat_a, mat_b), lambda x: x, entering
            )
            carried = from_behind(leaving, "section", 1)
    kept_normed = jnp.zeros((MICRO, micro_rows, D), jnp.bfloat16)
    kept_dpre = jnp.zeros((MICRO, micro_rows, RANK), jnp.bfloat16)
    kept_act = jnp.zeros((MICRO, micro_rows, RANK), jnp.bfloat16)
    kept_upper = jnp.zeros((MICRO, micro_rows, D), jnp.bfloat16)
    carried_grad = jnp.zeros((micro_rows, D), jnp.bfloat16)
    for turn in range(turns):
        micro = turn - (sections - 1 - here)
        active = (micro >= 0) & (micro < MICRO)
        picked = jnp.clip(micro, 0, MICRO - 1)
        last = lax.dynamic_slice_in_dim(cotangent, picked * micro_rows, micro_rows, 0)
        upstream = jnp.where(here == sections - 1, last, carried_grad)
        hidden = lax.dynamic_index_in_dim(saved, picked, 0, keepdims=False)

        def run_layer():
            return backward_layer(hidden, upstream, mat_a, mat_b)

        def skip_layer():
            return (
                upstream,
                jnp.zeros((micro_rows, D), jnp.bfloat16),
                jnp.zeros((micro_rows, RANK), jnp.bfloat16),
                jnp.zeros((micro_rows, RANK), jnp.bfloat16),
            )

        earlier, normed, dpre, act = lax.cond(active, run_layer, skip_layer)
        kept_normed = store(kept_normed, normed, picked, active)
        kept_dpre = store(kept_dpre, dpre, picked, active)
        kept_act = store(kept_act, act, picked, active)
        kept_upper = store(kept_upper, upstream, picked, active)
        if turn < turns - 1:
            carried_grad = from_behind(earlier, "section", -1)
    all_rows = MICRO * micro_rows
    terms_in = slot_grads(
        kept_normed.reshape(all_rows, D),
        kept_dpre.reshape(all_rows, RANK),
        all_in[0],
        rows_d,
        rows_k,
    )[None]
    terms_out = slot_grads(
        kept_act.reshape(all_rows, RANK),
        kept_upper.reshape(all_rows, D),
        all_out[0],
        rows_k,
        rows_d,
    )[None]
    sums_in, sums_out = (
        lax.psum_scatter(
            terms_in.astype(jnp.bfloat16), "dp", scatter_dimension=1, tiled=True
        ).astype(jnp.float32),
        lax.psum_scatter(
            terms_out.astype(jnp.bfloat16), "dp", scatter_dimension=1, tiled=True
        ).astype(jnp.float32),
    )
    return (sums_in.astype(jnp.bfloat16), sums_out.astype(jnp.bfloat16))


SLICES = 2
GATHER_PLANE = (1, 1)
REDUCE_PLANE = (1, 1)
CHUNK = 2048

def plain_order(depth):
    steps = []
    both = [d for r in range(1, depth) for d in (-r, r)]
    slices = range(SLICES)
    for k in slices:
        steps += [(name, k) for name in ("gs", "gf", "gu", "gd", "gp", "near")]
        steps += [("rows",)] if k == 0 else []
        steps += [("line", k, d) for d in both] + [("nline", k, d) for d in both]
        steps += [("pown", k)] + [("plane", k, d) for d in both] + [("side", k)]
        steps += [("tables",), ("scales",)] if k == 0 else []
        steps += [("expand", k, 0), ("expand", k, 1), ("middle", k), ("outer", k, 0), ("outer", k, 1)]
        steps += [("second", k, d, w) for d in range(depth) for w in (1, 0)]
    for k in slices:
        steps += [("lout", k, -d) for d in reversed(both)] + [("first", k, d) for d in range(depth)]
        steps += [("lsum", k), ("lfirst", k)] + [("zout", k, -d) for d in reversed(both)]
        steps += [("finish", k)]
    return steps + [("place", k) for k in slices]


ORDER = (
    ("gs", 0), ("gd", 0), ("gs", 1), ("gf", 0), ("gp", 0), ("rows",), ("gu", 0), ("near", 0),
    ("line", 0, 1), ("line", 0, -1), ("gf", 1), ("gu", 1), ("line", 0, -2), ("line", 0, 2),
    ("pown", 0), ("scales",), ("nline", 0, -1), ("line", 0, -3), ("nline", 0, 1),
    ("plane", 0, -1), ("line", 0, 3), ("plane", 0, 1), ("nline", 0, -2), ("nline", 0, 3),
    ("gd", 1), ("nline", 0, -3), ("plane", 0, -2), ("nline", 0, 2), ("plane", 0, 2), ("gp", 1),
    ("near", 1), ("line", 1, 1), ("plane", 0, -3), ("line", 1, -1), ("plane", 0, 3),
    ("side", 0), ("tables",), ("line", 1, 2), ("line", 1, -2), ("expand", 0, 0),
    ("nline", 1, 1), ("pown", 1), ("expand", 0, 1), ("nline", 1, -1), ("line", 1, 3),
    ("middle", 0), ("nline", 1, -2), ("plane", 1, 1), ("nline", 1, 2), ("line", 1, -3),
    ("plane", 1, -1), ("outer", 0, 0), ("nline", 1, -3), ("nline", 1, 3), ("outer", 0, 1),
    ("plane", 1, -2), ("plane", 1, 2), ("second", 0, 3, 1), ("lout", 0, -3), ("lout", 0, 3),
    ("second", 0, 1, 1), ("second", 0, 2, 1), ("side", 1), ("second", 0, 3, 0),
    ("second", 0, 1, 0), ("second", 0, 2, 0), ("plane", 1, 3), ("plane", 1, -3),
    ("expand", 1, 0), ("first", 0, 3), ("lout", 0, -2), ("lout", 0, 2), ("expand", 1, 1),
    ("first", 0, 1), ("middle", 1), ("lout", 0, -1), ("lout", 0, 1), ("first", 0, 2),
    ("outer", 1, 0), ("zout", 0, 3), ("outer", 1, 1), ("lout", 1, -3), ("second", 1, 3, 1),
    ("second", 1, 1, 1), ("second", 1, 2, 1), ("lout", 1, 3), ("second", 1, 1, 0),
    ("second", 1, 3, 0), ("zout", 0, -3), ("second", 1, 2, 0), ("lout", 1, -2), ("first", 1, 3),
    ("lout", 1, 2), ("first", 1, 1), ("second", 1, 0, 1), ("lout", 1, -1), ("zout", 1, -3),
    ("lout", 1, 1), ("zout", 0, 2), ("lsum", 0), ("zout", 1, 3), ("first", 1, 2),
    ("second", 0, 0, 1), ("zout", 0, -2), ("zout", 1, -2), ("zout", 0, 1), ("first", 1, 0),
    ("second", 0, 0, 0), ("lsum", 1), ("zout", 0, -1), ("zout", 1, 2), ("first", 0, 0),
    ("second", 1, 0, 0), ("zout", 1, -1), ("zout", 1, 1), ("lfirst", 0), ("lfirst", 1),
    ("finish", 0), ("finish", 1), ("place", 0), ("place", 1),
)


class Place:
    def __init__(self, devices):
        me = lax.axis_index("dp")
        self.depth = devices // 8
        self.me = me
        self.core = me % 2
        self.chip = me // 2
        x = self.chip % 2
        y = (self.chip // 2) % 2
        self.z = self.chip // 4
        dx = 1 - 2 * x
        dy = 2 * (1 - 2 * y)
        first = (1 - self.core) * dx + self.core * dy
        second = (1 - self.core) * dy + self.core * dx
        self.own = self.chip % 4
        self.near = self.own + first
        self.far = self.own + second
        self.diag = self.own + first + second
        self.sibling = me + 1 - 2 * self.core
        self.first = me + 2 * first
        self.second = me + 2 * second
        self.above = me + 8
        self.below = me - 8
        self.has_above = self.z + 1 < self.depth
        self.has_below = self.z >= 1

    def knock(self):
        barrier = pltpu.get_barrier_semaphore()

        def signal(peer):
            pl.semaphore_signal(
                barrier, inc=1, device_id={"dp": peer}, device_id_type=pl.DeviceIdType.MESH
            )

        for peer in (self.sibling, self.first, self.second):
            signal(peer)
        pl.when(self.has_above)(lambda: signal(self.above))
        pl.when(self.has_below)(lambda: signal(self.below))

        peers = 3 + self.has_above.astype(jnp.int32) + self.has_below.astype(jnp.int32)
        return lambda: pl.semaphore_wait(barrier, peers)


def remote(src, dst, send, recv, peer):
    return pltpu.make_async_remote_copy(
        src_ref=src,
        dst_ref=dst,
        send_sem=send,
        recv_sem=recv,
        device_id={"dp": peer},
        device_id_type=pl.DeviceIdType.MESH,
    )


class Layout:
    def __init__(self, devices, per, odd):
        self.split = per - odd
        self.depth = devices // 8
        self.sizes = (4 * (per - odd), 4 * odd)
        self.parts = (0, 1) if odd else (0,)
        self.plane = 16 * per
        self.total = self.depth * self.plane

    def part_of(self, j):
        return 0 if j < self.split else 1

    def first(self, part):
        return 0 if part == 0 else 2 * self.split

    def start(self, part, z, p):
        line, odd = self.sizes
        return z * self.plane + (p * line if part == 0 else 4 * line + p * odd)

    def piece(self, buf, k, part, z, p):
        span = pl.ds(self.start(part, z, p), self.sizes[part])
        return buf.at[span] if k is None else buf.at[k, span]

    def level(self, buf, k, z):
        line, odd = self.sizes
        span = pl.ds(z * self.plane + 4 * line, 4 * odd)
        return buf.at[span] if k is None else buf.at[k, span]


def fused_kernel(devices, pos_in, pos_out, blocks_in, blocks_out, tokens, cotangent, out,
                 own, full, stage, rows_h, rows_g, mats, grads, inverse,
                 tags, table, table_s, begin, begin_s, mid,
                 held, from_second, from_first, from_below, from_above, final, twin, flat,
                 load_sems, send_sems, group_sems, pair_sems, twin_sems, tag_sems, gather_sems, level_sems,
                 second_sems, first_sems, below_sems, above_sems):
    at = Place(devices)
    depth = at.depth
    core = at.core
    per = blocks_in.shape[0]
    gat = [Layout(devices, per, odd) for odd in GATHER_PLANE]
    red = [Layout(devices, per, odd) for odd in REDUCE_PLANE]
    count, width = tokens.shape
    size = full[0].shape[1]
    half = BLOCK // 2
    rows_k = RANK // BLOCK
    rows_d = width // BLOCK
    blocks = rows_k * rows_d
    ranks = rows_k * size
    chunks = width // CHUNK
    sends = []
    waits = []
    groups = {}
    singles = []

    def groups_at(name):
        return group_sems.at[groups[name]]


    def like(kind, rows):
        if kind == "tag":
            return tags.at[0]
        return tags.at[pl.ds(0, rows)] if kind == "tags" else full[0].at[pl.ds(0, rows)]

    def send(src, dst, recv, peer, present=None, group=None):
        whole = src.dtype == jnp.int32
        kind = ("tag" if len(src.shape) == 2 else "tags") if whole else "blocks"
        if group is not None:
            name, copies = group
            name += (kind,)
            if name not in groups:
                groups[name] = len(groups)
                sends.append((True, groups[name], kind, copies * src.shape[0], None))
            sem = groups_at(name)
        else:
            singles.append(present)
            sem = send_sems.at[len(singles) - 1]
            sends.append((False, len(singles) - 1, kind, src.shape[0], present))
        remote(src, dst, sem, recv, peer).start()

    def got(buf, sem):
        remote(buf, buf, send_sems.at[0], sem, at.sibling).wait_recv()

    wait_peers = at.knock()
    own_loads = [
        pltpu.make_async_copy(blocks_in, own.at[0], load_sems.at[5]),
        pltpu.make_async_copy(blocks_out, own.at[1], load_sems.at[6]),
    ]
    for copy in own_loads:
        copy.start()

    own_rows = pl.ds(pl.multiple_of(core * count, count), count)
    local = [
        pltpu.make_async_copy(tokens, rows_h.at[own_rows], load_sems.at[0]),
        pltpu.make_async_copy(cotangent, rows_g.at[own_rows], load_sems.at[1]),
    ]
    for copy in local:
        copy.start()

    lanes = lax.broadcasted_iota(jnp.int32, tags.shape[1:], 1)
    row = jnp.full(tags.shape[1:], 2 * blocks, jnp.int32)
    for j in range(per):
        place = pos_in[0, j]
        row = jnp.where(lanes == 2 * j, jnp.where(place < blocks, place, 2 * blocks), row)
        row = jnp.where(lanes == 2 * j + 1, pos_out[0, j] + blocks, row)
    tags[at.me] = row

    for copy in own_loads:
        copy.wait()
    for j in range(per):
        flat[0] = own[0, j].T
        flat[1] = own[1, j]
        for k in range(SLICES):
            lay = gat[k]
            part = lay.part_of(j)
            base = lay.start(part, at.z, at.own) + core * (lay.sizes[part] // 2)
            base += 2 * j - lay.first(part)
            keep = pl.ds(pl.multiple_of(core * half + k * size, size), size)
            give = pl.ds(pl.multiple_of((1 - core) * half + k * size, size), size)
            for m in range(2):
                full[k][base + m] = flat[m, keep, :]
                stage[k, 2 * j + m] = flat[m, give, :]
    for k in range(SLICES):
        full[k][gat[k].total] = jnp.zeros((size, BLOCK), jnp.bfloat16)
        grads[k][2 * blocks] = jnp.zeros((size, BLOCK), jnp.bfloat16)

    wait_peers()

    def pair(k, start):
        lay = gat[k]
        for part in lay.parts:
            n = lay.sizes[part] // 2
            base = lay.start(part, at.z, at.own) + core * n
            src, dst = stage.at[k, pl.ds(lay.first(part), n)], full[k].at[pl.ds(base, n)]
            if start:
                send(src, dst, pair_sems.at[k, part], at.sibling)
            else:
                got(src, pair_sems.at[k, part])

    send(tags.at[at.me], tags.at[at.me], tag_sems.at[4 * depth], at.sibling)
    for k in range(SLICES):
        pair(k, True)

    def tag_piece(z, p):
        return tags.at[pl.ds(2 * (4 * z + p), 2)]

    def push(k, part, z, p, peer, present=None):
        group = None
        if peer is at.second:
            group = (("gather", k, part, 2), 2 * depth if part == 0 else 2)
        elif peer is at.first:
            group = (("gather", k, part, 1), depth if part == 0 else 1)
        if k == 0 and part == 0:
            piece = tag_piece(z, p)
            send(piece, piece, tag_sems.at[4 * z + p], peer, present, group)
        piece = gat[k].piece(full[k], None, part, z, p)
        send(piece, piece, gather_sems.at[k, 4 * z + p if part == 0 else 4 * depth + p], peer, present, group)

    def arrived(k, part, z, p):
        if k == 0 and part == 0:
            got(tag_piece(z, p), tag_sems.at[4 * z + p])
        got(gat[k].piece(full[k], None, part, z, p), gather_sems.at[k, 4 * z + p if part == 0 else 4 * depth + p])

    def inside(d):
        return (at.z + d < depth) if d > 0 else (at.z + d >= 0)

    def onward(d):
        return (at.has_below, at.below) if d > 0 else (at.has_above, at.above)

    def away(d):
        return (at.has_above, at.above) if d > 0 else (at.has_below, at.below)

    def own_second(k):
        pair(k, False)
        if k == 0:
            got(tags.at[at.me], tag_sems.at[4 * depth])
        push(k, 0, at.z, at.own, at.second)

    def own_first(k):
        push(k, 0, at.z, at.own, at.first)

    def own_line(k, d):
        more, peer = away(d)
        pl.when(more)(lambda: push(k, 0, at.z, at.own, peer, lambda: more))

    def own_plane(k):
        for part in gat[k].parts[1:]:
            push(k, part, at.z, at.own, at.second)
            push(k, part, at.z, at.own, at.first)

    def near_own(k):
        for part in gat[k].parts:
            arrived(k, part, at.z, at.near)
            push(k, part, at.z, at.near, at.second)

    def line(k, d):
        more, peer = onward(d)
        here = inside(d)

        def run():
            z = at.z + d
            arrived(k, 0, z, at.own)
            pl.when(more)(lambda: push(k, 0, z, at.own, peer, lambda: more & here))
            push(k, 0, z, at.own, at.second, lambda: here)
            push(k, 0, z, at.own, at.first, lambda: here)

        pl.when(here)(run)

    def near_line(k, d):
        here = inside(d)

        def run():
            arrived(k, 0, at.z + d, at.near)
            push(k, 0, at.z + d, at.near, at.second, lambda: here)

        pl.when(here)(run)

    def push_level(k, z, peer, present):
        piece = gat[k].level(full[k], None, z)
        send(piece, piece, level_sems.at[k, z], peer, present)

    def plane_own(k):
        for part in gat[k].parts:
            for p in (at.far, at.diag):
                arrived(k, part, at.z, p)
        if gat[k].sizes[1]:
            for more, peer in (away(1), away(-1)):
                pl.when(more)(lambda more=more, peer=peer: push_level(k, at.z, peer, lambda: more))

    def plane(k, d):
        more, peer = onward(d)
        here = inside(d)

        def run():
            got(gat[k].level(full[k], None, at.z + d), level_sems.at[k, at.z + d])
            pl.when(more)(lambda: push_level(k, at.z + d, peer, lambda: more & here))

        if gat[k].sizes[1]:
            pl.when(here)(run)

    def side(k):
        for d in range(1 - depth, depth):

            def run(d=d):
                for p in (at.far, at.diag):
                    arrived(k, 0, at.z + d, p)

            if d:
                pl.when(inside(d))(run)

    def load_rows():
        swap = [
            remote(tokens, rows_h.at[own_rows], load_sems.at[7 + SLICES], load_sems.at[2], at.sibling),
            remote(cotangent, rows_g.at[own_rows], load_sems.at[8 + SLICES], load_sems.at[3], at.sibling),
        ]
        for copy in swap:
            copy.start()
        waits.extend(swap)

    def scales():
        for copy in local:
            copy.wait()
        for copy in waits:
            copy.wait_recv()
        total = jnp.zeros((2 * count, BLOCK), jnp.float32)
        for i in range(0, width, BLOCK):
            wide = rows_h[:, i : i + BLOCK].astype(jnp.float32)
            total += wide * wide
        scale = jnp.sqrt(jnp.sum(total, axis=-1, keepdims=True) / width + EPS)
        inverse[...] = jnp.broadcast_to(1.0 / scale, inverse.shape)

    def tables():
        table[...] = tags[:, 0, :]
        copy = pltpu.make_async_copy(table, table_s, load_sems.at[4])
        copy.start()
        copy.wait()
        shape = begin[0].shape
        numbers = lax.broadcasted_iota(jnp.int32, shape, 0) * BLOCK
        numbers += lax.broadcasted_iota(jnp.int32, shape, 1)

        kinds = {lay.split: lay for lay in gat}

        def scan(dev, found):
            z, p, which = dev // 8, (dev // 2) % 4, dev % 2
            bases = [
                [lay.start(part, z, p) + which * (lay.sizes[part] // 2) for part in range(2)]
                for lay in kinds.values()
            ]
            found = list(found)
            for lane in range(2 * per):
                same = numbers == table_s[dev, lane]
                for n, lay in enumerate(kinds.values()):
                    part = lay.part_of(lane // 2)
                    entry = bases[n][part] + (lane - lay.first(part))
                    found[n] = jnp.where(same, entry, found[n])
            return tuple(found)

        found = lax.fori_loop(
            0, devices, scan,
            tuple(jnp.full(shape, lay.total, jnp.int32) for lay in kinds.values()),
        )
        found = dict(zip(kinds, found))
        copies = []
        for k in range(SLICES):
            begin[k][...] = found[gat[k].split]
            copies.append(pltpu.make_async_copy(begin[k], begin_s[k], load_sems.at[7 + k]))
            copies[k].start()
        for copy in copies:
            copy.wait()

    def expand(k, m):
        group = BLOCK // rows_k

        def step(low, carry, high):
            r = high * group + low
            into = pl.ds(pl.multiple_of(r * BLOCK, BLOCK), BLOCK)
            found = []
            for c in range(rows_k):
                if m == 0:
                    at_c = begin_s[k][high, low * rows_k + c]
                else:
                    b = blocks + c * rows_d + high * group
                    at_c = begin_s[k][b // BLOCK, b % BLOCK + low]
                found.append(full[k][at_c])
            for c in range(rows_k):
                mats[m, c * size : (c + 1) * size, into] = found[c]
            return carry

        for high in range(rows_d // group):
            lax.fori_loop(0, group, functools.partial(step, high=high), 0, unroll=4)

    def product(m):
        rows = rows_h if m == 0 else rows_g
        total = jnp.zeros((2 * count, ranks), jnp.float32)
        for i in range(0, width, CHUNK):
            total += lax.dot_general(
                rows[:, i : i + CHUNK], mats[m, :, i : i + CHUNK],
                (((1,), (1,)), ((), ())), preferred_element_type=jnp.float32,
            )
        return total

    def middle(k):
        scale = inverse[:, :ranks] if ranks <= BLOCK else inverse[:, :1]
        pre = product(0) * scale
        dact = product(1)
        sig = jax.nn.sigmoid(pre)
        dpre = dact * sig * (1.0 + pre * (1.0 - sig))
        mid[0] = (dpre * scale).T.astype(jnp.bfloat16)
        mid[1] = (pre * sig).T.astype(jnp.bfloat16)

    def outer(k, m):
        rows = rows_h if m == 0 else rows_g

        def step(i, carry):
            into = pl.ds(pl.multiple_of(i * CHUNK, CHUNK), CHUNK)
            part = lax.dot_general(
                mid[m], rows[:, into], (((1,), (0,)), ((), ())), preferred_element_type=jnp.float32
            ).astype(jnp.bfloat16)
            for r in range(CHUNK // BLOCK):
                col = i * (CHUNK // BLOCK) + r
                for c in range(rows_k):
                    b = col * rows_k + c if m == 0 else blocks + c * rows_d + col
                    grads[k][b] = part[c * size : (c + 1) * size, r * BLOCK : (r + 1) * BLOCK]
            return carry

        lax.fori_loop(0, chunks, step, 0)

    def fill(k, part, z, p, terms, into=None):
        lay = red[k]
        n = lay.sizes[part] // 2
        first = lay.first(part)
        base = lay.start(part, z, p)

        def step(which, carry):
            dev = 2 * (4 * z + p) + which
            for i in range(n):
                entry = base + which * n + i
                value = grads[k][table_s[dev, first + i]]
                if terms:
                    value = value.astype(jnp.float32)
                    for term in terms:
                        value += term[k, entry].astype(jnp.float32)
                    value = value.astype(jnp.bfloat16)
                if into is None:
                    held[k, entry] = value
                else:
                    into[k, 2 * first + which * n + i] = value
            return carry

        lax.fori_loop(0, 2, step, 0)

    def give(k, part, z, p, buf, sem, peer, present=None):
        src = red[k].piece(held, k, part, z, p)
        group = None
        if peer is at.second:
            group = (("sums", k, part, 2), 2 * depth if part == 0 else 2)
        elif peer is at.first:
            group = (("sums", k, part, 1), depth if part == 0 else 1)
        send(src, red[k].piece(buf, k, part, z, p), sem, peer, present, group)

    def take(k, part, z, p, buf, sem):
        got(red[k].piece(buf, k, part, z, p), sem)

    def sem_second(k, part, z, passed):
        return second_sems.at[k, passed, z if part == 0 else depth]

    def sem_first(k, part, z):
        return first_sems.at[k, z if part == 0 else depth]

    def behind(d):
        if d > 0:
            return at.has_below, from_below, below_sems, at.above
        return at.has_above, from_above, above_sems, at.below

    def level_out(k, d):
        before, buf, sems, peer = behind(d)
        here = inside(d)

        def run():
            z = at.z + d

            def fills(terms):
                for p in range(4):
                    fill(k, 1, z, p, terms)

            def summed():
                got(red[k].level(buf, k, z), sems.at[k, 1, z])
                fills([buf])

            pl.when(jnp.logical_not(before))(lambda: fills([]))
            pl.when(before)(summed)
            send(
                red[k].level(held, k, z), red[k].level(buf, k, z), sems.at[k, 1, z],
                peer, lambda: here,
            )

        if red[k].sizes[1]:
            pl.when(here)(run)

    def beside(run):
        above, below = at.has_above, at.has_below
        pl.when(below & above)(lambda: run([from_below, from_above]))
        pl.when(below & jnp.logical_not(above))(lambda: run([from_below]))
        pl.when(above & jnp.logical_not(below))(lambda: run([from_above]))

    def second(k, d, which):
        z = (at.z + d) % depth
        p = at.diag if which else at.far
        fill(k, 0, z, p, [])
        give(k, 0, z, p, from_second, sem_second(k, 0, z, which), at.second)

    def first(k, d):
        z = (at.z + d) % depth
        take(k, 0, z, at.near, from_second, sem_second(k, 0, z, 1))
        fill(k, 0, z, at.near, [from_second])
        give(k, 0, z, at.near, from_first, sem_first(k, 0, z), at.first)

    def level_sums(k):
        if not red[k].sizes[1]:
            return
        for more, buf, sems in (
            (at.has_below, from_below, below_sems), (at.has_above, from_above, above_sems)
        ):
            pl.when(more)(
                lambda buf=buf, sems=sems: got(red[k].level(buf, k, at.z), sems.at[k, 1, at.z])
            )

        def run(terms):
            for p in (at.diag, at.far):
                fill(k, 1, at.z, p, terms)

        beside(run)
        for passed, p in ((1, at.diag), (0, at.far)):
            give(k, 1, at.z, p, from_second, sem_second(k, 1, at.z, passed), at.second)

    def level_first(k):
        if not red[k].sizes[1]:
            return
        take(k, 1, at.z, at.near, from_second, sem_second(k, 1, at.z, 1))
        beside(lambda terms: fill(k, 1, at.z, at.near, [from_second] + terms))
        give(k, 1, at.z, at.near, from_first, sem_first(k, 1, at.z), at.first)

    def line_out(k, d):
        before, buf, sems, peer = behind(d)
        here = inside(d)
        terms = [from_second, from_first]

        def run():
            z = at.z + d
            take(k, 0, z, at.own, from_second, sem_second(k, 0, z, 0))
            take(k, 0, z, at.own, from_first, sem_first(k, 0, z))

            def summed():
                take(k, 0, z, at.own, buf, sems.at[k, 0, z])
                fill(k, 0, z, at.own, terms + [buf])

            pl.when(jnp.logical_not(before))(lambda: fill(k, 0, z, at.own, terms))
            pl.when(before)(summed)
            give(k, 0, z, at.own, buf, sems.at[k, 0, z], peer, lambda: here)

        pl.when(here)(run)

    def finish(k):
        lay = red[k]
        for part in lay.parts[::-1]:
            take(k, part, at.z, at.own, from_second, sem_second(k, part, at.z, 0))
            take(k, part, at.z, at.own, from_first, sem_first(k, part, at.z))
        pl.when(at.has_below)(lambda: take(k, 0, at.z, at.own, from_below, below_sems.at[k, 0, at.z]))
        pl.when(at.has_above)(lambda: take(k, 0, at.z, at.own, from_above, above_sems.at[k, 0, at.z]))

        def run(terms):
            for part in lay.parts:
                fill(k, part, at.z, at.own, [from_second, from_first] + terms, final)

        beside(run)
        for part in lay.parts:
            n = lay.sizes[part] // 2
            piece = pl.ds(2 * lay.first(part) + (1 - core) * n, n)
            send(final.at[k, piece], twin.at[k, piece], twin_sems.at[k, part], at.sibling)

    def assemble(k):
        lay = red[k]
        for part in lay.parts:
            n = lay.sizes[part] // 2
            piece = pl.ds(2 * lay.first(part) + core * n, n)
            got(twin.at[k, piece], twin_sems.at[k, part])
        mine = pl.ds(pl.multiple_of(core * half + k * size, size), size)
        theirs = pl.ds(pl.multiple_of((1 - core) * half + k * size, size), size)
        for j in range(per):
            part = lay.part_of(j)
            entry = lay.first(part) + core * (lay.sizes[part] // 2) + 2 * j
            flat[j, mine, :] = final[k, entry]
            flat[j, theirs, :] = twin[k, entry]
            out[1, j, mine, :] = final[k, entry + 1]
            out[1, j, theirs, :] = twin[k, entry + 1]

    steps = {
        "gs": own_second, "gf": own_first, "gu": lambda k: own_line(k, 1),
        "gd": lambda k: own_line(k, -1), "gp": own_plane, "rows": load_rows,
        "near": near_own, "line": line, "nline": near_line, "pown": plane_own, "plane": plane,
        "side": side, "tables": tables, "scales": scales, "expand": expand, "middle": middle,
        "outer": outer, "lout": level_out, "second": second, "first": first,
        "lsum": level_sums, "lfirst": level_first, "zout": line_out, "finish": finish,
        "place": assemble,
    }
    for step in ORDER if depth == 4 else plain_order(depth):
        steps[step[0]](*step[1:])
    for j in range(per):
        out[0, j] = flat[j].T
    for shared, n, kind, rows, present in sends:

        def sent(shared=shared, n=n, kind=kind, rows=rows):
            piece = like(kind, rows)
            sem = group_sems.at[n] if shared else send_sems.at[n]
            remote(piece, piece, sem, load_sems.at[0], at.sibling).wait_send()

        if present is None:
            sent()
        else:
            pl.when(present())(sent)
    for copy in waits:
        copy.wait_send()


def one_section(tokens, blocks_in, blocks_out, pos_in, pos_out, cotangent):
    devices = lax.axis_size("dp")
    per = blocks_in.shape[1]
    count, width = tokens.shape
    depth = devices // 8
    chips = devices // 2
    entries = 4 * per * chips
    sends = 1 + 2 * depth + SLICES * 8 * depth
    shared = 8 * SLICES + 2
    size = BLOCK // 2 // SLICES
    ranks = RANK // BLOCK * size
    blocks = (width // BLOCK) * (RANK // BLOCK)
    dma = pltpu.SemaphoreType.DMA
    vmem = pltpu.VMEM
    anywhere = pl.BlockSpec(memory_space=pl.ANY)
    scalars = pl.BlockSpec(memory_space=pltpu.SMEM)
    local = pl.BlockSpec(memory_space=vmem)
    bf16, f32, i32 = jnp.bfloat16, jnp.float32, jnp.int32
    shards = (SLICES, entries, size, BLOCK)
    words = -(-(2 * blocks + 1) // BLOCK)
    words = -(-words // 8) * 8
    results = pl.pallas_call(
        functools.partial(fused_kernel, devices),
        out_shape=jax.ShapeDtypeStruct((2, per, BLOCK, BLOCK), bf16),
        in_specs=[scalars, scalars] + [anywhere] * 4,
        out_specs=local,
        scratch_shapes=[
            vmem((2, per, BLOCK, BLOCK), bf16),
            [vmem((entries + 1, size, BLOCK), bf16) for _ in range(SLICES)],
            vmem((SLICES, 2 * per, size, BLOCK), bf16),
            vmem((2 * count, width), bf16),
            vmem((2 * count, width), bf16),
            vmem((2, ranks, width), bf16),
            [vmem((2 * blocks + 1, size, BLOCK), bf16) for _ in range(SLICES)],
            vmem((2 * count, BLOCK), f32),
            vmem((devices, 8, BLOCK), i32),
            vmem((devices, BLOCK), i32),
            pltpu.SMEM((devices, BLOCK), i32),
            [vmem((words, BLOCK), i32) for _ in range(SLICES)],
            [pltpu.SMEM((words, BLOCK), i32) for _ in range(SLICES)],
            vmem((2, ranks, 2 * count), bf16),
            vmem(shards, bf16),
            vmem(shards, bf16),
            vmem(shards, bf16),
            vmem(shards, bf16),
            vmem(shards, bf16),
            vmem((SLICES, 4 * per, size, BLOCK), bf16),
            vmem((SLICES, 4 * per, size, BLOCK), bf16),
            vmem((per, BLOCK, BLOCK), bf16),
            dma((9 + SLICES,)),
            dma((sends,)),
            dma((shared,)),
            dma((SLICES, 2)),
            dma((SLICES, 2)),
            dma((chips + 1,)),
            dma((SLICES, chips + 4)),
            dma((SLICES, depth)),
            dma((SLICES, 2, depth + 1)),
            dma((SLICES, depth + 1)),
            dma((SLICES, 2, depth)),
            dma((SLICES, 2, depth)),
        ],
        compiler_params=pltpu.CompilerParams(
            collective_id=0, has_side_effects=True, vmem_limit_bytes=63 * 1024 * 1024
        ),
        name="fused_adapters",
    )(pos_in, pos_out, blocks_in[0], blocks_out[0], tokens, cotangent)
    return (results[0][None], results[1][None])


def solution(mesh):
    in_specs = (
        P("dp", None),
        P("section", "dp", None, None),
        P("section", "dp", None, None),
        P("section", "dp"),
        P("section", "dp"),
        P("dp", None),
    )
    out_specs = (P("section", "dp", None, None), P("section", "dp", None, None))
    body = one_section if mesh.shape["section"] == 1 else per_device
    return jax.shard_map(
        body, mesh=mesh, in_specs=in_specs, out_specs=out_specs, check_vma=False
    )
```
